256 devices in a mesh: ctx: 16 (over y, x_lo, core), ch: 16 (over z, x_hi).
Axes of the slice: x: 4 (x_hi: 2, x_lo: 2; x = x_hi * 2 + x_lo), y: 4, z: 8, core: 2. Of those that a mesh axis runs over, the one named last changes fastest.
Arguments:
- hidden_in: bfloat16 [16384, 4096], P('ctx', 'ch'), may hold values from -6 to 6
- in_weight: bfloat16 [3, 4096, 4096], P(None, None, 'ch'), may hold values from -0.09375 to 0.09375
- out_weight: bfloat16 [4096, 4096], P('ch'), may hold values from -0.125 to 0.125
- decay: float32 [4096, 16], P('ch'), may hold values from 1.5258789e-05 to 0.0061035156
- residue: float32 [4096, 16], P('ch'), may hold values from -0.0234375 to 0.0234375
- skip_gain: float32 [4096], P('ch'), may hold values from -4 to 4
- block_order: int32 [32], replicated, may hold values from 0 to 31, each once
Outputs:
- layer_out: bfloat16 [16384, 4096], P('ctx', 'ch')
The draws below stay inside these ranges and needn't reach their ends.
Inputs may be any that keep to these rules, and one draw needn't show every extreme that they name: `block_order`: every half-block of the sequence stands in exactly one slot.
All inputs are finite; a program needn't handle non-finite values.
Results may differ from the reference program's by a relative error of at most 0.012.
Values may be sent and summed in bfloat16 or wider, within the bound.
No kernel may reach another device: no remote copies, remote signals or barrier semaphores. Data moves between devices by JAX's collectives and lax.ppermute only.
A program may use at most 128 MiB of HBM per device.

```python
import math
import jax
import jax.numpy as jnp

D = 4096
ORDER = 16
TOK_DEV = 1024
SEQ = 16384
N_CTX = 16


def raised(result, rng, source, target, parts, factor):
    owner, partner = [(jnp.arange(result.shape[position]) // (result.shape[position] // parts)).reshape([-1 if axis == position else 1 for axis in range(result.ndim)]) for position in (source, target)]
    chosen = jax.random.permutation(rng, parts)[partner]
    strong = (owner == chosen) | (owner == (partner + parts // 2) % parts)
    return jnp.where(strong, factor * result, result)


def level_of(rng, dims, split, least, top_value):
    loudness = 1.0
    for dim, parts in split:
        draws = jax.random.uniform(jax.random.fold_in(jax.random.fold_in(rng, 6), dim), (parts,), jnp.float32, least / len(split), top_value / len(split))
        loudness = loudness * jnp.repeat(jnp.exp(draws), dims[dim] // parts).reshape((-1,) + (1,) * (len(dims) - 1 - dim))
    return loudness


def noise(rng, shape, deviation, most, cuts=(), dtype=jnp.bfloat16):
    result = deviation * jax.random.normal(rng, shape, jnp.float32)
    if cuts:
        result = result * level_of(rng, shape, cuts, -0.22, 0.18)
    return jnp.clip(result, -most, most).astype(dtype)


def gaussian_with(key, shape, scale, most, cuts, heavy, dtype=jnp.bfloat16):
    entries = scale * jax.random.normal(key, shape, jnp.float32)
    if cuts:
        entries = entries * level_of(key, shape, cuts, -0.22, 0.18)
    return jnp.clip(raised(entries, jax.random.fold_in(key, 3), *heavy), -most, most).astype(dtype)


def setup_inputs(seed: int = 0) -> dict:
    arg_keys = jax.random.split(jax.random.key(seed), 8)
    hidden_in = noise(arg_keys[0], (SEQ, D), 1.0, 6.0, ((0, 16), (1, 16)))
    in_weight = noise(arg_keys[1], (3, D, D), D ** -0.5, 0.09375, ((2, 16),))
    out_weight = gaussian_with(arg_keys[2], (D, D), D ** -0.5, 0.125, ((0, 16),), (0, 1, 16, 2.0))
    decay = jnp.clip(jnp.exp(math.log(0.0061035156) - 5.9914645 * jax.random.uniform(arg_keys[3], (D, ORDER), jnp.float32) ** level_of(arg_keys[3], (D, ORDER), ((0, 16),), -0.2, 0.2)), 1.52587890625e-05, 0.0061035156)
    residue = noise(arg_keys[4], (D, ORDER), (ORDER * SEQ // 4) ** -0.5, 0.0234375, ((0, 16),), jnp.float32)
    skip_gain = noise(arg_keys[5], (D,), 1.0, 4.0, ((0, 16),), jnp.float32)
    block_order = jax.random.permutation(arg_keys[6], 2 * N_CTX).astype(jnp.int32)
    return dict(hidden_in=hidden_in, in_weight=in_weight, out_weight=out_weight, decay=decay, residue=residue, skip_gain=skip_gain, block_order=block_order)


def reference(hidden_in, in_weight, out_weight, decay, residue, skip_gain, block_order):
    streams = [jnp.dot(hidden_in, in_weight[j], preferred_element_type=jnp.float32).astype(jnp.bfloat16) for j in range(3)]
    query_rows, key_rows, value_rows = streams
    mixed_in = (key_rows.astype(jnp.float32) * value_rows.astype(jnp.float32)).astype(jnp.bfloat16)
    slot_rows = mixed_in.astype(jnp.float32).reshape(2 * N_CTX, TOK_DEV // 2, D)
    natural = jnp.zeros_like(slot_rows).at[block_order.astype(jnp.int32)].set(slot_rows).reshape(SEQ, D)
    lag_times = jnp.arange(SEQ).astype(jnp.float32)[:, None]
    tap_values = jnp.zeros((SEQ, D), jnp.float32)
    for mode_index in range(ORDER):
        tap_values = tap_values + residue[:, mode_index][None, :] * jnp.exp(-decay[:, mode_index][None, :] * lag_times)
    length = 2 * SEQ
    spectrum = jnp.fft.rfft(natural, n=length, axis=0) * jnp.fft.rfft(tap_values, n=length, axis=0)
    conv_rows = jnp.fft.irfft(spectrum, n=length, axis=0)[:SEQ].astype(jnp.float32)
    slot_conv = conv_rows.reshape(2 * N_CTX, TOK_DEV // 2, D)[block_order.astype(jnp.int32)].reshape(SEQ, D)
    gated = (query_rows.astype(jnp.float32) * (slot_conv + skip_gain[None, :] * mixed_in.astype(jnp.float32))).astype(jnp.bfloat16)
    return jnp.dot(gated, out_weight, preferred_element_type=jnp.float32).astype(jnp.bfloat16)
```

```python
import jax
import jax.numpy as jnp
from jax import lax
from jax.experimental import pallas as pl
from jax.experimental.pallas import tpu as pltpu
from jax.sharding import Mesh
from jax.sharding import PartitionSpec as P

F32 = jnp.float32
BF16 = jnp.bfloat16
SWAP = [(0, 1), (1, 0)]
ORDER = 16
SEGS = 8
ANY = pl.BlockSpec(memory_space=pl.ANY)
SMEM = pl.BlockSpec(memory_space=pltpu.SMEM)
VMEM = pl.BlockSpec(memory_space=pltpu.VMEM)


def around(size, step):
    return [(i, (i + step) % size) for i in range(size)]


def spread(chunk, axis, size, ahead, behind):
    forward = backward = chunk
    chunks, offsets = [chunk], [0]
    for hop in range(1, max(ahead, behind) + 1):
        if hop <= ahead:
            forward = lax.ppermute(forward, axis, around(size, 1))
            chunks.append(forward)
            offsets.append(-hop)
        if hop <= behind:
            backward = lax.ppermute(backward, axis, around(size, -1))
            chunks.append(backward)
            offsets.append(hop)
    return chunks, offsets


def load_rows_and_weights(where, chunks, weights, streams, rows, weight_rows, sems):
    width = chunks[0].shape[1]
    copies = []
    for i, chunk in enumerate(chunks):
        place = pl.multiple_of(where[i] * width, width)
        copies.append(pltpu.make_async_copy(chunk, rows.at[:, pl.ds(place, width)], sems.at[i]))
    base = len(chunks)
    if len(weights) == 1:
        for k, j in enumerate(streams):
            copies.append(pltpu.make_async_copy(weights[0].at[j], weight_rows.at[k], sems.at[base + k]))
    else:
        deep = weights[0].shape[1]
        for k, j in enumerate(streams):
            for i, part in enumerate(weights):
                place = pl.multiple_of(where[base + i] * deep, deep)
                copies.append(
                    pltpu.make_async_copy(
                        part.at[j],
                        weight_rows.at[k, pl.ds(place, deep), :],
                        sems.at[base + k * len(weights) + i],
                    )
                )
    for copy in copies:
        copy.start()
    return copies


def project_query(where, *refs, n_chunks, n_weights):
    chunks, weights = refs[:n_chunks], refs[n_chunks : n_chunks + n_weights]
    query, rows, weight_rows, sems = refs[n_chunks + n_weights :]
    for copy in load_rows_and_weights(where, chunks, weights, (0,), rows, weight_rows, sems):
        copy.wait()
    query[...] = jnp.dot(rows[...], weight_rows[0], preferred_element_type=F32).astype(BF16)


def project_mixed(where, *refs, n_chunks, n_weights):
    chunks, weights = refs[:n_chunks], refs[n_chunks : n_chunks + n_weights]
    rates, mixed, ends, state, rows, weight_rows, mixed_rows, sems = refs[n_chunks + n_weights :]
    copies = load_rows_and_weights(where, chunks, weights, (1, 2), rows, weight_rows, sems)
    for copy in copies:
        copy.wait()
    keys = jnp.dot(rows[...], weight_rows[0], preferred_element_type=F32).astype(BF16)
    values = jnp.dot(rows[...], weight_rows[1], preferred_element_type=F32).astype(BF16)
    product = (keys.astype(F32) * values.astype(F32)).astype(BF16)
    mixed[...] = product
    tokens, width = mixed.shape
    for g in range(width // 128):
        mixed_rows[g] = product[:, g * 128 : (g + 1) * 128].astype(F32)
    steps = tokens // SEGS
    fall = jnp.exp(-rates[...])
    later = (SEGS - 1 - lax.broadcasted_iota(jnp.int32, (SEGS, 128), 0)).astype(F32) * float(steps)
    for g in range(width // 128):
        lanes = slice(g * 128, (g + 1) * 128)
        falls = [jnp.broadcast_to(fall[n : n + 1, lanes], (SEGS, 128)) for n in range(ORDER)]

        def step(t, states, g=g, falls=falls):
            now = mixed_rows[g, pl.ds(t, SEGS, stride=steps), :]
            return tuple(f * s + now for f, s in zip(falls, states))

        states = lax.fori_loop(
            0, steps, step, tuple(jnp.zeros((SEGS, 128), F32) for _ in range(ORDER)), unroll=4
        )
        for n in range(ORDER):
            ends[n, :, lanes] = states[n]
            weight = jnp.exp(-rates[n : n + 1, lanes] * later)
            state[n : n + 1, lanes] = jnp.sum(weight * states[n], axis=0, keepdims=True)


def convolve_and_project(where, lags, *refs, n_pieces, n_parts):
    pieces = refs[:n_pieces]
    (ends_own, ends_peer, mixed_own, mixed_peer, query_own, query_peer, rates, gains, skip, out_own) = refs[
        n_pieces : n_pieces + 10
    ]
    parts = refs[n_pieces + 10 : n_pieces + 10 + n_parts]
    partial, mixed_rows, conv_rows, gated = refs[n_pieces + 10 + n_parts :]
    tokens, half = mixed_own.shape
    width = 2 * half
    steps = tokens // SEGS
    for g in range(width // 128):
        source = mixed_own if g * 128 < half else mixed_peer
        mixed_rows[g] = source[:, g * 128 % half : g * 128 % half + 128].astype(F32)
    rate = rates[...]
    incoming = jnp.zeros((ORDER, width), F32)
    slot = 0
    for piece in pieces:
        for i in range(piece.shape[0]):
            lag = lags[slot]
            live = (lag >= 0.0).astype(F32)
            incoming = incoming + live * jnp.exp(-rate * jnp.maximum(lag, 0.0)) * piece[i]
            slot += 1
    fall = jnp.exp(-rate)
    gain = gains[...]
    order = lax.broadcasted_iota(jnp.int32, (SEGS, 128), 0)
    before = order.astype(F32) * float(steps)
    for g in range(width // 128):
        lanes = slice(g * 128, (g + 1) * 128)
        ends = ends_own if g * 128 < half else ends_peer
        end_lanes = slice(g * 128 % half, g * 128 % half + 128)
        starts = []
        for n in range(ORDER):
            total = ends[n, :, end_lanes]
            slow = rate[n : n + 1, lanes]
            for reach in (1, 2, 4):
                moved = jnp.where(order >= reach, pltpu.roll(total, reach, 0), 0.0)
                total = total + jnp.exp(-slow * float(reach * steps)) * moved
            total = jnp.where(order >= 1, pltpu.roll(total, 1, 0), 0.0)
            starts.append(total + jnp.exp(-slow * before) * incoming[n : n + 1, lanes])
        falls = [jnp.broadcast_to(fall[n : n + 1, lanes], (SEGS, 128)) for n in range(ORDER)]
        rises = [jnp.broadcast_to(gain[n : n + 1, lanes], (SEGS, 128)) for n in range(ORDER)]

        def step(t, states, g=g, falls=falls, rises=rises):
            now = mixed_rows[g, pl.ds(t, SEGS, stride=steps), :]
            states = tuple(f * s + now for f, s in zip(falls, states))
            terms = [r * s for r, s in zip(rises, states)]
            while len(terms) > 1:
                terms = [a + b for a, b in zip(terms[::2], terms[1::2])]
            conv_rows[g, pl.ds(t, SEGS, stride=steps), :] = terms[0]
            return states

        lax.fori_loop(0, steps, step, tuple(starts), unroll=2)
    for g in range(width // 128):
        query = query_own if g * 128 < half else query_peer
        lanes = slice(g * 128, (g + 1) * 128)
        inner = conv_rows[g] + skip[:, lanes] * mixed_rows[g]
        gated[:, lanes] = (query[:, g * 128 % half : g * 128 % half + 128].astype(F32) * inner).astype(BF16)
    cols = parts[0].shape[1]
    for i, part in enumerate(parts):
        k = where[i]
        place = pl.multiple_of(k * cols, cols)
        own = jnp.dot(gated[:, :half], out_own[:, pl.ds(place, cols)], preferred_element_type=F32)
        peer = jnp.dot(gated[:, half:], part[...], preferred_element_type=F32)
        partial[k] = (own + peer).astype(BF16)


def per_device(hidden_in, in_weight, out_weight, decay, residue, skip_gain, block_order):
    y, xl, core = lax.axis_index("y"), lax.axis_index("xl"), lax.axis_index("core")
    z, xh = lax.axis_index("z"), lax.axis_index("xh")
    n_y, n_z = lax.axis_size("y"), lax.axis_size("z")
    tok_rows, width = hidden_in.shape
    features = in_weight.shape[1]
    tokens = tok_rows // 2
    n_parts = n_y * 2

    mine = lax.dynamic_slice_in_dim(hidden_in, xh * tokens, tokens, 0)
    others = lax.dynamic_slice_in_dim(hidden_in, (1 - xh) * tokens, tokens, 0)
    from_peer = lax.ppermute(others, "xh", SWAP)
    own_chunks, own_off = spread(mine, "z", n_z, 4, 3)
    peer_chunks, peer_off = spread(from_peer, "z", n_z, 3, 4)
    chunk_at = [((z + o) % n_z) * 2 + xh for o in own_off] + [((z + o) % n_z) * 2 + 1 - xh for o in peer_off]
    chunks = own_chunks + peer_chunks

    small = jnp.concatenate([decay.T, residue.T, skip_gain[None]], 0)
    small = jnp.concatenate([small, lax.ppermute(small, "xh", SWAP)], 1)
    rates, gains, skip = small[:ORDER], small[ORDER : 2 * ORDER], small[2 * ORDER :]
    part = y * 2 + core
    deep = features // n_parts
    in_part = lax.dynamic_slice_in_dim(in_weight, part * deep, deep, 1)
    out_cols = features // n_parts
    out_part = lax.dynamic_slice_in_dim(out_weight, part * out_cols, out_cols, 1)
    in_parts, part_off = spread(lax.ppermute(in_part, "xh", SWAP), "y", n_y, 2, 1)
    in_parts = in_parts + [lax.ppermute(p, "core", SWAP) for p in in_parts]
    out_parts, _ = spread(lax.ppermute(out_part, "xh", SWAP), "y", n_y, 2, 1)
    out_parts = out_parts + [lax.ppermute(p, "core", SWAP) for p in out_parts]
    part_at = [((y + o) % n_y) * 2 + core for o in part_off] + [((y + o) % n_y) * 2 + 1 - core for o in part_off]
    where = jnp.stack(chunk_at + part_at).astype(jnp.int32)
    where_parts = jnp.stack(part_at).astype(jnp.int32)

    def project(kernel, weights, n_streams, extra, out_shape, scratch):
        return pl.pallas_call(
            kernel,
            in_specs=[SMEM] + [ANY] * (len(chunks) + len(weights)) + [VMEM] * len(extra),
            out_specs=jax.tree.map(lambda _: VMEM, out_shape),
            out_shape=out_shape,
            scratch_shapes=[
                pltpu.VMEM((tokens, features), BF16),
                pltpu.VMEM((n_streams, features, width), BF16),
                *scratch,
                pltpu.SemaphoreType.DMA((len(chunks) + n_streams * len(weights),)),
            ],
            compiler_params=pltpu.CompilerParams(vmem_limit_bytes=48 << 20),
        )(where, *chunks, *weights, *extra)

    def query(weights):
        def kernel(*refs):
            project_query(*refs, n_chunks=len(chunks), n_weights=len(weights))

        return project(kernel, weights, 1, [], jax.ShapeDtypeStruct((tokens, width), BF16), [])

    def mixed(weights, rate):
        def kernel(*refs):
            project_mixed(*refs, n_chunks=len(chunks), n_weights=len(weights))

        shapes = (
            jax.ShapeDtypeStruct((tokens, width), BF16),
            jax.ShapeDtypeStruct((ORDER, SEGS, width), F32),
            jax.ShapeDtypeStruct((ORDER, width), F32),
        )
        return project(kernel, weights, 2, [rate], shapes, [pltpu.VMEM((width // 128, tokens, 128), F32)])

    mixed_own, ends_own, state_own = mixed([in_weight], rates[:, :width])
    mixed_peer, ends_peer, state_peer = mixed(in_parts, rates[:, width:])
    query_own = query([in_weight])
    query_peer = query(in_parts)

    own_first = jnp.concatenate([state_own, state_peer], 1)
    peer_first = jnp.concatenate([state_peer, state_own], 1)
    states = jnp.stack([own_first, lax.ppermute(peer_first, "xh", SWAP)])
    slots = jnp.stack([xh, 1 - xh])
    states = jnp.concatenate([states, lax.ppermute(states, "core", SWAP)])
    slots = jnp.concatenate([slots + 2 * core, slots + 2 * (1 - core)])
    states = jnp.concatenate([states, lax.ppermute(states, "xl", SWAP)])
    slots = jnp.concatenate([slots + 4 * xl, slots + 4 * (1 - xl)])
    pieces = [states] + [lax.ppermute(states, "y", around(n_y, s)) for s in (1, -1, 2)]
    slots = jnp.concatenate([slots + 8 * ((y + o) % n_y) for o in (0, -1, 1, -2)])
    here = jnp.sum(jnp.where(jnp.arange(block_order.shape[0]) == 2 * (4 * y + 2 * xl + core) + xh, block_order, 0))
    there = jnp.sum(
        jnp.where(jnp.arange(block_order.shape[0])[None] == slots[:, None], block_order[None], 0), axis=1
    )
    lags = ((here - 1 - there) * tokens).astype(F32)

    partial = pl.pallas_call(
        lambda *refs: convolve_and_project(*refs, n_pieces=len(pieces), n_parts=n_parts),
        in_specs=[SMEM, SMEM] + [VMEM] * (len(pieces) + 10 + n_parts),
        out_specs=VMEM,
        out_shape=jax.ShapeDtypeStruct((n_parts, tokens, out_cols), BF16),
        scratch_shapes=[
            pltpu.VMEM((2 * width // 128, tokens, 128), F32),
            pltpu.VMEM((2 * width // 128, tokens, 128), F32),
            pltpu.VMEM((tokens, 2 * width), BF16),
        ],
        compiler_params=pltpu.CompilerParams(vmem_limit_bytes=48 << 20),
    )(
        where_parts,
        lags,
        *pieces,
        ends_own,
        ends_peer,
        mixed_own,
        mixed_peer,
        query_own,
        query_peer,
        rates,
        gains,
        skip,
        out_weight,
        *out_parts,
    )

    def share(offset, rows):
        return lax.dynamic_index_in_dim(partial, (z + offset) % n_z, 0, keepdims=False)[rows]

    def collect(rows, ahead, behind):
        forward, backward = share(ahead, rows), share(-behind, rows)
        for hop in range(max(ahead, behind), 0, -1):
            if hop <= ahead:
                forward = lax.ppermute(forward, "z", around(n_z, 1)).astype(F32)
                if hop > 1:
                    forward = (forward + share(hop - 1, rows).astype(F32)).astype(BF16)
            if hop <= behind:
                backward = lax.ppermute(backward, "z", around(n_z, -1)).astype(F32)
                if hop > 1:
                    backward = (backward + share(1 - hop, rows).astype(F32)).astype(BF16)
        return forward + backward + share(0, rows).astype(F32)

    total = jnp.concatenate(
        [collect(slice(0, tokens // 2), 4, 3), collect(slice(tokens // 2, tokens), 3, 4)], 0
    ).astype(BF16)
    keep = lax.dynamic_slice_in_dim(total, xh * width, width, 1)
    give = lax.dynamic_slice_in_dim(total, (1 - xh) * width, width, 1)
    take = lax.ppermute(give, "xh", SWAP)
    first = xh == 0
    return jnp.concatenate([jnp.where(first, keep, take), jnp.where(first, take, keep)], 0)


def solution(mesh):
    ctx, ch = ("y", "xl", "core"), ("z", "xh")
    grid = Mesh(mesh.devices.reshape(4, 2, 2, 8, 2), ctx + ch)
    placed = (
        P(ctx, ch),
        P(None, None, ch),
        P(ch, None),
        P(ch, None),
        P(ch, None),
        P(ch),
        P(),
    )
    return jax.shard_map(
        per_device, mesh=grid, in_specs=placed, out_specs=P(ctx, ch), check_vma=False
    )
```

```python
import jax
import jax.numpy as jnp
from jax import lax
from jax.experimental import pallas as pl
from jax.experimental.pallas import tpu as pltpu
from jax.sharding import Mesh
from jax.sharding import PartitionSpec as P

F32 = jnp.float32
BF16 = jnp.bfloat16
SWAP = [(0, 1), (1, 0)]
ORDER = 16
SEGS = 8
HBM = pl.BlockSpec(memory_space=pltpu.HBM)
SMEM = pl.BlockSpec(memory_space=pltpu.SMEM)
VMEM = pl.BlockSpec()


def around(size, step):
    return [(i, (i + step) % size) for i in range(size)]


DEPTH = 1024


def project(where, chunks, weights, streams, rows, weight_rows, sums, sems):
    width = chunks[0].shape[1]
    features = rows.shape[1]
    for i, chunk in enumerate(chunks):
        place = pl.multiple_of(where[i] * width, width)
        pltpu.make_async_copy(chunk, rows.at[:, pl.ds(place, width)], sems.at[0]).start()
    held = weights if len(weights) > 1 else []
    for k, j in enumerate(streams):
        if not held:
            pltpu.make_async_copy(weights[0].at[j], weight_rows.at[k], sems.at[1 + k]).start()
        for i, part in enumerate(held):
            deep = part.shape[1]
            place = pl.multiple_of(where[len(chunks) + i] * deep, deep)
            block = weight_rows.at[k, pl.ds(place, deep), :]
            pltpu.make_async_copy(part.at[k], block, sems.at[1 + k]).start()
    sums[...] = jnp.zeros(sums.shape, F32)
    pltpu.make_async_copy(rows, rows, sems.at[0]).wait()

    def stream(k, _):
        pltpu.make_async_copy(weight_rows.at[k], weight_rows.at[k], sems.at[1 + k]).wait()

        def step(i, _):
            at = pl.multiple_of(i * DEPTH, DEPTH)
            sums[k] += jnp.dot(
                rows[:, pl.ds(at, DEPTH)], weight_rows[k, pl.ds(at, DEPTH), :], preferred_element_type=F32
            )
            return 0

        return lax.fori_loop(0, features // DEPTH, step, 0)

    lax.fori_loop(0, len(streams), stream, 0)


def project_query(where, *refs, n_chunks, n_weights):
    chunks, weights = refs[:n_chunks], refs[n_chunks : n_chunks + n_weights]
    query, rows, weight_rows, sums, sems = refs[n_chunks + n_weights :]
    project(where, chunks, weights, (0,), rows, weight_rows, sums, sems)
    query[...] = sums[0].astype(BF16)


def project_mixed(where, *refs, n_chunks, n_weights, streams):
    chunks, weights = refs[:n_chunks], refs[n_chunks : n_chunks + n_weights]
    rates = refs[n_chunks + n_weights]
    outs = refs[n_chunks + n_weights + 1 : -5]
    rows, weight_rows, sums, mixed_rows, sems = refs[-5:]
    mixed, ends, state = outs[:3]
    tokens, width = mixed.shape
    steps = tokens // SEGS
    project(where, chunks, weights, streams, rows, weight_rows, sums, sems)
    keys, values = sums[streams.index(1)].astype(BF16), sums[streams.index(2)].astype(BF16)
    if 0 in streams:
        outs[3][...] = sums[streams.index(0)].astype(BF16)
    product = (keys.astype(F32) * values.astype(F32)).astype(BF16)
    mixed[...] = product
    for g in range(width // 128):
        mixed_rows[g] = product[:, g * 128 : (g + 1) * 128].astype(F32)
    fall = jnp.exp(-rates[...])
    later = (SEGS - 1 - lax.broadcasted_iota(jnp.int32, (SEGS, 128), 0)).astype(F32) * float(steps)
    for g in range(width // 128):
        lanes = slice(g * 128, (g + 1) * 128)
        falls = [jnp.broadcast_to(fall[n : n + 1, lanes], (SEGS, 128)) for n in range(ORDER)]

        def step(t, states, g=g, falls=falls):
            now = mixed_rows[g, pl.ds(t, SEGS, stride=steps), :]
            return tuple(f * s + now for f, s in zip(falls, states))

        states = lax.fori_loop(
            0, steps, step, tuple(jnp.zeros((SEGS, 128), F32) for _ in range(ORDER)), unroll=4
        )
        for n in range(ORDER):
            ends[n, :, lanes] = states[n]
            weight = jnp.exp(-rates[n : n + 1, lanes] * later)
            state[n : n + 1, lanes] = jnp.sum(weight * states[n], axis=0, keepdims=True)


def pass_on(lags, *refs, n_pieces):
    pieces, rates, outs = refs[:n_pieces], refs[n_pieces], refs[n_pieces + 1 :]
    rate = -rates[...]
    per_piece = pieces[0].shape[0]
    for k, out in enumerate(outs):
        total = jnp.zeros(rate.shape, F32)
        for p, piece in enumerate(pieces):
            for i in range(per_piece):
                lag = lags[(k * n_pieces + p) * per_piece + i]
                live = (lag >= 0.0).astype(F32)
                total = total + live * (jnp.exp(rate * jnp.maximum(lag, 0.0)) * piece[i])
        out[...] = total


def convolve_and_project(where, *refs, n_given, n_parts, n_outs):
    given = refs[:n_given]
    ends, mixed, query = [refs[n_given + 2 * i : n_given + 2 * i + 2] for i in range(3)]
    rates, gains, skip, out_own = refs[n_given + 6 : n_given + 10]
    parts = refs[n_given + 10 : n_given + 10 + n_parts]
    outs = refs[n_given + 10 + n_parts : n_given + 10 + n_parts + n_outs]
    mixed_rows, conv_rows, gated, own_cols, peer_cols, stage, sems = refs[n_given + 10 + n_parts + n_outs :]
    tokens, half = mixed[0].shape
    width = 2 * half
    steps = tokens // SEGS
    cols = own_cols.shape[1] // peer_cols.shape[0]
    held = [part.at[1] for part in parts]
    pltpu.make_async_copy(out_own, own_cols, sems.at[0]).start()
    for i, part in enumerate(held):
        for j in (0, 1):
            lanes = pl.ds(j * half, half)
            pltpu.make_async_copy(part.at[lanes, :], peer_cols.at[where[i], :, lanes], sems.at[1]).start()
    for g in range(width // 128):
        source = mixed[g * 128 // half]
        mixed_rows[g] = source[:, g * 128 % half : g * 128 % half + 128].astype(F32)
    incoming = given[0][...]
    for more in given[1:]:
        incoming = incoming + more[...]
    rate = rates[...]
    fall = jnp.exp(-rate)
    gain = gains[...]
    order = lax.broadcasted_iota(jnp.int32, (SEGS, 128), 0)
    before = order.astype(F32) * float(steps)
    for g in range(width // 128):
        lanes = slice(g * 128, (g + 1) * 128)
        end_lanes = slice(g * 128 % half, g * 128 % half + 128)
        starts = []
        for n in range(ORDER):
            total = ends[g * 128 // half][n, :, end_lanes]
            slow = rate[n : n + 1, lanes]
            for reach in (1, 2, 4):
                moved = jnp.where(order >= reach, pltpu.roll(total, reach, 0), 0.0)
                total = total + jnp.exp(-slow * float(reach * steps)) * moved
            total = jnp.where(order >= 1, pltpu.roll(total, 1, 0), 0.0)
            starts.append(total + jnp.exp(-slow * before) * incoming[n : n + 1, lanes])
        falls = [jnp.broadcast_to(fall[n : n + 1, lanes], (SEGS, 128)) for n in range(ORDER)]
        rises = [jnp.broadcast_to(gain[n : n + 1, lanes], (SEGS, 128)) for n in range(ORDER)]

        def step(t, states, g=g, falls=falls, rises=rises):
            now = mixed_rows[g, pl.ds(t, SEGS, stride=steps), :]
            states = tuple(f * s + now for f, s in zip(falls, states))
            terms = [r * s for r, s in zip(rises, states)]
            while len(terms) > 1:
                terms = [a + b for a, b in zip(terms[::2], terms[1::2])]
            conv_rows[g, pl.ds(t, SEGS, stride=steps), :] = terms[0]
            return states

        lax.fori_loop(0, steps, step, tuple(starts), unroll=2)
        inner = conv_rows[g] + skip[:, lanes] * mixed_rows[g]
        gated[:, lanes] = (query[g * 128 // half][:, end_lanes].astype(F32) * inner).astype(BF16)
    pltpu.make_async_copy(own_cols, own_cols, sems.at[0]).wait()
    pltpu.make_async_copy(peer_cols, peer_cols, sems.at[1]).wait()

    def block(i, _):
        k = where[len(held) + i]
        place = pl.multiple_of(k * cols, cols)
        own = jnp.dot(gated[:, :half], own_cols[:, pl.ds(place, cols)], preferred_element_type=F32)
        peer = jnp.dot(gated[:, half:], peer_cols[k], preferred_element_type=F32)
        stage[i] = (own + peer).astype(BF16)
        return 0

    copies = []
    for first in range(0, n_outs // 2, 4):
        lax.fori_loop(first, first + 4, block, 0)
        for i in range(2 * first, 2 * first + 8):
            rows = pl.ds(i % 2 * (tokens // 2), tokens // 2)
            copies.append(pltpu.make_async_copy(stage.at[i // 2, rows, :], outs[i], sems.at[2 + i]))
            copies[-1].start()
    for copy in copies:
        copy.wait()


def per_device(hidden_in, in_weight, out_weight, decay, residue, skip_gain, block_order):
    y, xl, core = lax.axis_index("y"), lax.axis_index("xl"), lax.axis_index("core")
    z, xh = lax.axis_index("z"), lax.axis_index("xh")
    n_y, n_z = lax.axis_size("y"), lax.axis_size("z")
    tok_rows, width = hidden_in.shape
    features = in_weight.shape[1]
    tokens = tok_rows // 2
    n_parts = n_y * 2

    mine = lax.dynamic_slice_in_dim(hidden_in, xh * tokens, tokens, 0)
    others = lax.dynamic_slice_in_dim(hidden_in, (1 - xh) * tokens, tokens, 0)
    small = jnp.concatenate([decay.T, residue.T, skip_gain[None]], 0)
    part = y * 2 + core
    deep = out_cols = features // n_parts

    def mixed_part(p):
        return lax.dynamic_slice(in_weight, (1, p * deep, 0), (2, deep, width))

    def rest_part(p):
        query = lax.dynamic_slice(in_weight, (0, p * deep, 0), (1, deep, width))
        left = lax.dynamic_slice(out_weight, (0, p * out_cols), (width, width))
        right = lax.dynamic_slice(out_weight, (0, p * out_cols + width), (width, width))
        return jnp.concatenate([query, jnp.concatenate([left, right], 0)[None]], 0)

    def swap(piece, axis="xh"):
        return lax.ppermute(piece, axis, SWAP)

    def pass_around(piece, axis, size):
        return lax.ppermute(piece, axis, around(size, 1)), lax.ppermute(piece, axis, around(size, -1))

    far_part = (part + n_parts // 2) % n_parts
    together = lax.optimization_barrier
    own, peer, small_peer = together((pass_around(mine, "z", n_z), swap(others), swap(small)))
    own_f, own_b = [mine, own[0]], [mine, own[1]]
    peer_f, peer_b = [peer], [peer]
    own, peer, mixed_near = together(
        (
            (lax.ppermute(own_f[-1], "z", around(n_z, 1)), lax.ppermute(own_b[-1], "z", around(n_z, -1))),
            pass_around(peer, "z", n_z),
            swap(mixed_part(part)),
        )
    )
    for seq, got in zip((own_f, own_b, peer_f, peer_b), own + peer):
        seq.append(got)
    own, peer, mixed_side, mixed_far = together(
        (
            (lax.ppermute(own_f[-1], "z", around(n_z, 1)), lax.ppermute(own_b[-1], "z", around(n_z, -1))),
            (lax.ppermute(peer_f[-1], "z", around(n_z, 1)), lax.ppermute(peer_b[-1], "z", around(n_z, -1))),
            pass_around(mixed_near, "y", n_y),
            swap(mixed_part(far_part)),
        )
    )
    for seq, got in zip((own_f, own_b, peer_f, peer_b), own + peer):
        seq.append(got)
    mixed_parts = [mixed_near, mixed_far, *mixed_side]
    own, peer, mixed_there, rest_near = together(
        (
            (lax.ppermute(own_f[-1], "z", around(n_z, 1)),),
            (lax.ppermute(peer_f[-1], "z", around(n_z, 1)), lax.ppermute(peer_b[-1], "z", around(n_z, -1))),
            [swap(p, "core") for p in mixed_parts],
            swap(rest_part(part)),
        )
    )
    for seq, got in zip((own_f, peer_f, peer_b), own + peer):
        seq.append(got)
    mixed_parts = mixed_parts + mixed_there
    last = lax.ppermute(peer_b[-1], "z", around(n_z, -1))
    rest_side, rest_far = pass_around(rest_near, "y", n_y), swap(rest_part(far_part))
    peer_b.append(last)
    rest_parts = [rest_near, rest_far, *rest_side]
    rest_parts = rest_parts + [swap(p, "core") for p in rest_parts]
    small = jnp.concatenate([small, small_peer], 1)
    rates, gains, skip = small[:ORDER], small[ORDER : 2 * ORDER], small[2 * ORDER :]
    chunks = own_f + own_b[1:] + peer_f + peer_b[1:]
    chunk_at = [((z + o) % n_z) * 2 + xh for o in (0, -1, -2, -3, -4, 1, 2, 3)]
    chunk_at += [((z + o) % n_z) * 2 + 1 - xh for o in (0, -1, -2, -3, 1, 2, 3, 4)]
    part_at = [((y + o) % n_y) * 2 + c for c in (core, 1 - core) for o in (0, 2, -1, 1)]
    where = jnp.stack(chunk_at + part_at).astype(jnp.int32)
    reach = [4, -3, 3, 2, -2, 1, -1, 0]
    where_out = jnp.stack(part_at + [(z + r) % n_z for r in reach]).astype(jnp.int32)

    def projection(kernel, weights, streams, extra, out_shape, scratch):
        return pl.pallas_call(
            kernel,
            in_specs=[SMEM] + [HBM] * (len(chunks) + len(weights)) + [VMEM] * len(extra),
            out_specs=jax.tree.map(lambda _: VMEM, out_shape),
            out_shape=out_shape,
            scratch_shapes=[
                pltpu.VMEM((tokens, features), BF16),
                pltpu.VMEM((streams, features, width), BF16),
                pltpu.VMEM((streams, tokens, width), F32),
                *scratch,
                pltpu.SemaphoreType.DMA((1 + streams,)),
            ],
            compiler_params=pltpu.CompilerParams(vmem_limit_bytes=60 << 20),
        )(where, *chunks, *weights, *extra)

    row_shape = jax.ShapeDtypeStruct((tokens, width), BF16)
    end_shape = jax.ShapeDtypeStruct((ORDER, SEGS, width), F32)
    state_shape = jax.ShapeDtypeStruct((ORDER, width), F32)
    group_rows = [pltpu.VMEM((width // 128, tokens, 128), F32)]
    mixed_own, ends_own, state_own, query_own = projection(
        lambda *refs: project_mixed(*refs, n_chunks=len(chunks), n_weights=1, streams=(1, 2, 0)),
        [in_weight],
        3,
        [rates[:, :width]],
        (row_shape, end_shape, state_shape, row_shape),
        group_rows,
    )
    mixed_peer, ends_peer, state_peer = projection(
        lambda *refs: project_mixed(*refs, n_chunks=len(chunks), n_weights=len(mixed_parts), streams=(1, 2)),
        mixed_parts,
        2,
        [rates[:, width:]],
        (row_shape, end_shape, state_shape),
        group_rows,
    )
    query_peer = projection(
        lambda *refs: project_query(*refs, n_chunks=len(chunks), n_weights=len(rest_parts)),
        rest_parts,
        1,
        [],
        row_shape,
        [],
    )
    state = jnp.concatenate([state_own, state_peer], 1)
    state, rest_parts = lax.optimization_barrier((state, rest_parts))

    pair = jnp.stack([state, lax.ppermute(state, "core", SWAP)])
    turned = jnp.concatenate([pair[:, :, width:], pair[:, :, :width]], 2)
    pieces = [
        pair,
        lax.ppermute(pair, "xl", SWAP),
        lax.ppermute(turned, "xh", SWAP),
        lax.ppermute(turned, ("xl", "xh"), [(0, 3), (3, 0), (1, 2), (2, 1)]),
    ]
    slots = jnp.stack(
        [
            8 * y + 4 * (xl ^ dl) + 2 * (core ^ dc) + (xh ^ dh)
            for dl, dh in ((0, 0), (1, 0), (0, 1), (1, 1))
            for dc in (0, 1)
        ]
    )
    ahead = [0, 1, -1, 2]
    targets = jnp.stack([8 * ((y + o) % n_y) + 4 * xl + 2 * core + xh for o in ahead])
    names = jnp.arange(block_order.shape[0])

    def place_of(which):
        return jnp.sum(jnp.where(names[None] == which[:, None], block_order[None], 0), axis=1)

    lags = ((place_of(targets)[:, None] - 1 - place_of(slots)[None]) * tokens).astype(F32).reshape(-1)
    given = pl.pallas_call(
        lambda *refs: pass_on(*refs, n_pieces=len(pieces)),
        in_specs=[SMEM] + [VMEM] * (len(pieces) + 1),
        out_specs=[VMEM] * len(ahead),
        out_shape=[jax.ShapeDtypeStruct(state.shape, F32)] * len(ahead),
    )(lags, *pieces, rates)
    given = [given[0]] + [lax.ppermute(g, "y", around(n_y, o)) for g, o in zip(given[1:], ahead[1:])]

    n_outs = 2 * len(reach)
    outs = pl.pallas_call(
        lambda *refs: convolve_and_project(*refs, n_given=len(given), n_parts=len(rest_parts), n_outs=n_outs),
        in_specs=[SMEM] + [VMEM] * (len(given) + 9) + [HBM] * (1 + len(rest_parts)),
        out_specs=[HBM] * n_outs,
        out_shape=[jax.ShapeDtypeStruct((tokens // 2, out_cols), BF16)] * n_outs,
        scratch_shapes=[
            pltpu.VMEM((2 * width // 128, tokens, 128), F32),
            pltpu.VMEM((2 * width // 128, tokens, 128), F32),
            pltpu.VMEM((tokens, 2 * width), BF16),
            pltpu.VMEM(out_weight.shape, BF16),
            pltpu.VMEM((n_parts, width, out_cols), BF16),
            pltpu.VMEM((len(reach), tokens, out_cols), BF16),
            pltpu.SemaphoreType.DMA((2 + n_outs,)),
        ],
        compiler_params=pltpu.CompilerParams(vmem_limit_bytes=60 << 20),
    )(
        where_out,
        *given,
        ends_own,
        ends_peer,
        mixed_own,
        mixed_peer,
        query_own,
        query_peer,
        rates,
        gains,
        skip,
        out_weight,
        *rest_parts,
    )
    share = {(r % n_z, h): outs[2 * i + h] for i, r in enumerate(reach) for h in (0, 1)}

    def collect(h, ahead, behind):
        forward, backward = share[ahead, h], share[-behind % n_z, h]
        for hop in range(max(ahead, behind), 0, -1):
            if hop <= ahead:
                forward = lax.ppermute(forward, "z", around(n_z, 1)).astype(F32)
                if hop > 1:
                    forward = (forward + share[hop - 1, h].astype(F32)).astype(BF16)
            if hop <= behind:
                backward = lax.ppermute(backward, "z", around(n_z, -1)).astype(F32)
                if hop > 1:
                    backward = (backward + share[(1 - hop) % n_z, h].astype(F32)).astype(BF16)
        total = (forward + backward + share[0, h].astype(F32)).astype(BF16)
        keep = lax.dynamic_slice_in_dim(total, xh * width, width, 1)
        give = lax.dynamic_slice_in_dim(total, (1 - xh) * width, width, 1)
        return keep, lax.ppermute(give, "xh", SWAP)

    keep, take = zip(collect(0, 4, 3), collect(1, 3, 4))
    first = xh == 0
    upper = [jnp.where(first, k, t) for k, t in zip(keep, take)]
    lower = [jnp.where(first, t, k) for k, t in zip(keep, take)]
    return jnp.concatenate(upper + lower, 0)


def solution(mesh):
    ctx, ch = ("y", "xl", "core"), ("z", "xh")
    grid = Mesh(mesh.devices.reshape(4, 2, 2, 8, 2), ctx + ch)
    placed = (
        P(ctx, ch),
        P(None, None, ch),
        P(ch, None),
        P(ch, None),
        P(ch, None),
        P(ch),
        P(),
    )
    return jax.shard_map(
        per_device, mesh=grid, in_specs=placed, out_specs=P(ctx, ch), check_vma=False
    )
```

```python
import jax
import jax.numpy as jnp
from jax import lax
from jax.experimental import pallas as pl
from jax.experimental.pallas import tpu as pltpu
from jax.sharding import Mesh
from jax.sharding import PartitionSpec as P

F32 = jnp.float32
BF16 = jnp.bfloat16
SWAP = [(0, 1), (1, 0)]
ORDER = 16
SEGS = 8
HBM = pl.BlockSpec(memory_space=pltpu.HBM)
SMEM = pl.BlockSpec(memory_space=pltpu.SMEM)
VMEM = pl.BlockSpec()


def around(size, step):
    return [(i, (i + step) % size) for i in range(size)]


GROUP = 4


def project_all(where, *refs, n_chunks):
    chunks = refs[:n_chunks]
    parts, (own, rates, mixed, ends, state, query) = refs[n_chunks : n_chunks + 2], refs[n_chunks + 2 : n_chunks + 8]
    rows, own_rows, peer_rows, own_sums, peer_sums, mixed_rows, sems = refs[n_chunks + 8 :]
    tokens, width = chunks[0].shape
    steps = tokens // SEGS
    for i, chunk in enumerate(chunks):
        pltpu.make_async_copy(chunk, rows.at[where[i]], sems.at[i]).start()
        block = pl.ds(pl.multiple_of(where[i] * width, width), width)
        for k, j in enumerate((1, 2, 0)):
            target = own_rows.at[i, :, pl.ds(k * width, width)]
            pltpu.make_async_copy(own.at[j, block, :], target, sems.at[n_chunks + i]).start()
    for p, part in enumerate(parts):
        blocks = pl.ds(pl.multiple_of(where[n_chunks + p], part.shape[1]), part.shape[1])
        for k in range(part.shape[0]):
            target = peer_rows.at[blocks, :, pl.ds(k * width, width)]
            pltpu.make_async_copy(part.at[k], target, sems.at[2 * n_chunks]).start()

    def own_step(g, _):
        total = None
        for j in range(GROUP):
            i = GROUP * g + j
            pltpu.make_async_copy(rows.at[0], rows.at[0], sems.at[i]).wait()
            pltpu.make_async_copy(own_rows.at[0], own_rows.at[0], sems.at[n_chunks + i]).wait()
            term = jnp.dot(rows[where[i]], own_rows[i], preferred_element_type=F32)
            total = term if total is None else total + term
        own_sums[...] += total
        return 0

    def peer_step(g, _):
        total = None
        for j in range(GROUP):
            term = jnp.dot(rows[GROUP * g + j], peer_rows[GROUP * g + j], preferred_element_type=F32)
            total = term if total is None else total + term
        peer_sums[...] += total
        return 0

    own_sums[...] = jnp.zeros(own_sums.shape, F32)
    peer_sums[...] = jnp.zeros(peer_sums.shape, F32)
    lax.fori_loop(0, n_chunks // GROUP, own_step, 0)
    pltpu.make_async_copy(peer_rows, peer_rows, sems.at[2 * n_chunks]).wait()
    lax.fori_loop(0, n_chunks // GROUP, peer_step, 0)
    for half, sums in enumerate((own_sums, peer_sums)):
        keys, values = sums[:, :width].astype(BF16), sums[:, width : 2 * width].astype(BF16)
        product = (keys.astype(F32) * values.astype(F32)).astype(BF16)
        place = slice(half * width, (half + 1) * width)
        mixed[:, place] = product
        for g in range(width // 128):
            mixed_rows[half * width // 128 + g] = product[:, g * 128 : (g + 1) * 128].astype(F32)
    query[...] = own_sums[:, 2 * width :].astype(BF16)
    fall = jnp.exp(-rates[...])
    later = (SEGS - 1 - lax.broadcasted_iota(jnp.int32, (SEGS, 128), 0)).astype(F32) * float(steps)
    for g in range(2 * width // 128):
        lanes = slice(g * 128, (g + 1) * 128)
        falls = [jnp.broadcast_to(fall[n : n + 1, lanes], (SEGS, 128)) for n in range(ORDER)]

        def step(t, states, g=g, falls=falls):
            now = mixed_rows[g, pl.ds(t, SEGS, stride=steps), :]
            return tuple(f * s + now for f, s in zip(falls, states))

        states = lax.fori_loop(
            0, steps, step, tuple(jnp.zeros((SEGS, 128), F32) for _ in range(ORDER)), unroll=4
        )
        for n in range(ORDER):
            ends[n, :, lanes] = states[n]
            weight = jnp.exp(-rates[n : n + 1, lanes] * later)
            state[n : n + 1, lanes] = jnp.sum(weight * states[n], axis=0, keepdims=True)


def project_query(where, *refs, n_chunks):
    chunks, parts = refs[:n_chunks], refs[n_chunks : n_chunks + 2]
    query, rows, weight_rows, sems = refs[n_chunks + 2 :]
    for p, part in enumerate(parts):
        blocks = pl.ds(pl.multiple_of(where[n_chunks + p], part.shape[1]), part.shape[1])
        pltpu.make_async_copy(part.at[0], weight_rows.at[blocks], sems.at[n_chunks]).start()
    for i, chunk in enumerate(chunks):
        pltpu.make_async_copy(chunk, rows.at[i], sems.at[i]).start()
    pltpu.make_async_copy(weight_rows, weight_rows, sems.at[n_chunks]).wait()
    total = jnp.zeros(query.shape, F32)
    for g in range(0, n_chunks, GROUP):
        for i in range(g, g + GROUP):
            pltpu.make_async_copy(rows.at[i], rows.at[i], sems.at[i]).wait()
        for i in range(g, g + GROUP):
            total += jnp.dot(rows[i], weight_rows[where[i]], preferred_element_type=F32)
    query[...] = total.astype(BF16)


def pass_on(lags, *refs, n_pieces):
    pieces, rates, outs = refs[:n_pieces], refs[n_pieces], refs[n_pieces + 1 :]
    rate = -rates[...]
    per_piece = pieces[0].shape[0]
    for k, out in enumerate(outs):
        total = jnp.zeros(rate.shape, F32)
        for p, piece in enumerate(pieces):
            for i in range(per_piece):
                lag = lags[(k * n_pieces + p) * per_piece + i]
                live = (lag >= 0.0).astype(F32)
                total = total + live * (jnp.exp(rate * jnp.maximum(lag, 0.0)) * piece[i])
        out[...] = total


def convolve_and_project(where, *refs, n_given, n_parts, n_outs):
    given = refs[:n_given]
    ends, mixed, query_own, query_peer, rates, gains, skip, out_own = refs[n_given : n_given + 8]
    parts = refs[n_given + 8 : n_given + 8 + n_parts]
    outs = refs[n_given + 8 + n_parts : n_given + 8 + n_parts + n_outs]
    mixed_rows, conv_rows, gated, own_cols, peer_cols, stage, sems = refs[n_given + 8 + n_parts + n_outs :]
    tokens, width = mixed.shape
    half = width // 2
    steps = tokens // SEGS
    cols = outs[0].shape[1]
    deep = parts[0].shape[1]
    pltpu.make_async_copy(out_own, own_cols, sems.at[0]).start()
    for i, part in enumerate(parts):
        target = peer_cols.at[:, pl.ds(pl.multiple_of(where[i] * deep, deep), deep)]
        pltpu.make_async_copy(part, target, sems.at[1]).start()
    for g in range(width // 128):
        mixed_rows[g] = mixed[:, g * 128 : (g + 1) * 128].astype(F32)
    incoming = given[0][...]
    for more in given[1:]:
        incoming = incoming + more[...]
    rate = rates[...]
    fall = jnp.exp(-rate)
    gain = gains[...]
    order = lax.broadcasted_iota(jnp.int32, (SEGS, 128), 0)
    before = order.astype(F32) * float(steps)
    for g in range(width // 128):
        lanes = slice(g * 128, (g + 1) * 128)
        starts = []
        for n in range(ORDER):
            total = ends[n, :, lanes]
            slow = rate[n : n + 1, lanes]
            for reach in (1, 2, 4):
                moved = jnp.where(order >= reach, pltpu.roll(total, reach, 0), 0.0)
                total = total + jnp.exp(-slow * float(reach * steps)) * moved
            total = jnp.where(order >= 1, pltpu.roll(total, 1, 0), 0.0)
            starts.append(total + jnp.exp(-slow * before) * incoming[n : n + 1, lanes])
        falls = [jnp.broadcast_to(fall[n : n + 1, lanes], (SEGS, 128)) for n in range(ORDER)]
        rises = [jnp.broadcast_to(gain[n : n + 1, lanes], (SEGS, 128)) for n in range(ORDER)]

        def step(t, states, g=g, falls=falls, rises=rises):
            now = mixed_rows[g, pl.ds(t, SEGS, stride=steps), :]
            states = tuple(f * s + now for f, s in zip(falls, states))
            terms = [r * s for r, s in zip(rises, states)]
            while len(terms) > 1:
                terms = [a + b for a, b in zip(terms[::2], terms[1::2])]
            conv_rows[g, pl.ds(t, SEGS, stride=steps), :] = terms[0]
            return states

        lax.fori_loop(0, steps, step, tuple(starts), unroll=2)
        inner = conv_rows[g] + skip[:, lanes] * mixed_rows[g]
        query = (query_own, query_peer)[g * 128 // half]
        gated[:, lanes] = (query[:, g * 128 % half : g * 128 % half + 128].astype(F32) * inner).astype(BF16)
    pltpu.make_async_copy(own_cols, own_cols, sems.at[0]).wait()
    pltpu.make_async_copy(peer_cols, peer_cols, sems.at[1]).wait()

    def block(i, _):
        k = where[len(parts) + i]
        place = pl.multiple_of(k * cols, cols)
        own = jnp.dot(gated[:, :half], own_cols[:, pl.ds(place, cols)], preferred_element_type=F32)
        peer = jnp.dot(gated[:, half:], peer_cols[:, pl.ds(place, cols)], preferred_element_type=F32)
        stage[i] = (own + peer).astype(BF16)
        return 0

    copies = []
    for first in (0, 4):
        lax.fori_loop(first, first + 4, block, 0)
        for i in range(first, first + 4):
            for out, rows in ((outs[0], pl.ds(0, tokens // 2)), (outs[1], pl.ds(tokens // 2, tokens // 2))):
                if i > 0:
                    out, rows = outs[i + 1], pl.ds(0, tokens)
                if i == 0 or len(copies) < i + 2:
                    copies.append(pltpu.make_async_copy(stage.at[i, rows, :], out, sems.at[2 + len(copies)]))
                    copies[-1].start()
    for copy in copies:
        copy.wait()


def per_device(hidden_in, in_weight, out_weight, decay, residue, skip_gain, block_order):
    y, xl, core = lax.axis_index("y"), lax.axis_index("xl"), lax.axis_index("core")
    z, xh = lax.axis_index("z"), lax.axis_index("xh")
    n_y, n_z = lax.axis_size("y"), lax.axis_size("z")
    tok_rows, width = hidden_in.shape
    features = in_weight.shape[1]
    tokens = tok_rows // 2

    mine = lax.dynamic_slice_in_dim(hidden_in, xh * tokens, tokens, 0)
    others = lax.dynamic_slice_in_dim(hidden_in, (1 - xh) * tokens, tokens, 0)
    small = jnp.concatenate([decay.T, residue.T, skip_gain[None]], 0)
    out_cols = features // n_z

    def swap(piece, axis="xh"):
        return lax.ppermute(piece, axis, SWAP)

    together = lax.optimization_barrier

    def ahead_z(x):
        return lax.ppermute(x, "z", around(n_z, 1))

    def back_z(x):
        return lax.ppermute(x, "z", around(n_z, -1))

    half, blocks = features // 2, features // 2 // width
    at = core * half
    mixed_part = lax.dynamic_slice(in_weight, (1, at, 0), (2, half, width)).reshape(2, blocks, width, width)
    of1, ob1, p0, small_peer, mixed_part = together(
        (ahead_z(mine), back_z(mine), swap(others), swap(small), mixed_part)
    )
    mixed_part = swap(mixed_part)
    of2, ob2, pf1, pb1 = together((ahead_z(of1), back_z(ob1), ahead_z(p0), back_z(p0)))
    of3, ob3, pf2, pb2 = together((ahead_z(of2), back_z(ob2), ahead_z(pf1), back_z(pb1)))
    of4, pf3, pb3, at = together((ahead_z(of3), ahead_z(pf2), back_z(pb2), at))
    query_part = lax.dynamic_slice(in_weight, (0, at, 0), (1, half, width)).reshape(1, blocks, width, width)
    pb4, mixed_part, query_part, at = together((back_z(pb3), mixed_part, query_part, at))
    query_part = swap(query_part)
    in_parts = [mixed_part, swap(mixed_part, "core")]
    out_part = lax.dynamic_slice_in_dim(out_weight, at, half, 1)
    small = jnp.concatenate([small, small_peer], 1)
    rates, gains, skip = small[:ORDER], small[ORDER : 2 * ORDER], small[2 * ORDER :]
    chunks = [mine, of1, of2, of3, of4, ob1, ob2, ob3, p0, pf1, pf2, pf3, pb1, pb2, pb3, pb4]
    chunk_at = [((z + o) % n_z) * 2 + xh for o in (0, -1, -2, -3, -4, 1, 2, 3)]
    chunk_at += [((z + o) % n_z) * 2 + 1 - xh for o in (0, -1, -2, -3, 1, 2, 3, 4)]
    part_at = [core * blocks, (1 - core) * blocks]
    where = jnp.stack(chunk_at + part_at).astype(jnp.int32)
    reach = [4, -3, 3, 2, -2, 1, -1, 0]
    where_out = jnp.stack([core, 1 - core] + [(z + r) % n_z for r in reach]).astype(jnp.int32)

    params = pltpu.CompilerParams(vmem_limit_bytes=60 << 20)
    mixed, ends, state, query_own = pl.pallas_call(
        lambda *refs: project_all(*refs, n_chunks=len(chunks)),
        in_specs=[SMEM] + [HBM] * (len(chunks) + 3) + [VMEM],
        out_specs=[VMEM] * 4,
        out_shape=[
            jax.ShapeDtypeStruct((tokens, 2 * width), BF16),
            jax.ShapeDtypeStruct((ORDER, SEGS, 2 * width), F32),
            jax.ShapeDtypeStruct((ORDER, 2 * width), F32),
            jax.ShapeDtypeStruct((tokens, width), BF16),
        ],
        scratch_shapes=[
            pltpu.VMEM((len(chunks), tokens, width), BF16),
            pltpu.VMEM((len(chunks), width, 3 * width), BF16),
            pltpu.VMEM((len(chunks), width, 2 * width), BF16),
            pltpu.VMEM((tokens, 3 * width), F32),
            pltpu.VMEM((tokens, 2 * width), F32),
            pltpu.VMEM((2 * width // 128, tokens, 128), F32),
            pltpu.SemaphoreType.DMA((2 * len(chunks) + 1,)),
        ],
        compiler_params=params,
    )(where, *chunks, *in_parts, in_weight, rates)

    pair = jnp.stack([state, lax.ppermute(state, "core", SWAP)])
    turned = jnp.concatenate([pair[:, :, width:], pair[:, :, :width]], 2)
    pieces = [
        pair,
        lax.ppermute(pair, "xl", SWAP),
        lax.ppermute(turned, "xh", SWAP),
        lax.ppermute(turned, ("xl", "xh"), [(0, 3), (3, 0), (1, 2), (2, 1)]),
    ]
    query_part, out_part, pieces = together((query_part, out_part, pieces))
    out_part = swap(out_part)
    query_peer = pl.pallas_call(
        lambda *refs: project_query(*refs, n_chunks=len(chunks)),
        in_specs=[SMEM] + [HBM] * (len(chunks) + 2),
        out_specs=VMEM,
        out_shape=jax.ShapeDtypeStruct((tokens, width), BF16),
        scratch_shapes=[
            pltpu.VMEM((len(chunks), tokens, width), BF16),
            pltpu.VMEM((len(chunks), width, width), BF16),
            pltpu.SemaphoreType.DMA((len(chunks) + 1,)),
        ],
        compiler_params=params,
    )(where, *chunks, query_part, swap(query_part, "core"))
    slots = jnp.stack(
        [
            8 * y + 4 * (xl ^ dl) + 2 * (core ^ dc) + (xh ^ dh)
            for dl, dh in ((0, 0), (1, 0), (0, 1), (1, 1))
            for dc in (0, 1)
        ]
    )
    ahead = [0, 1, -1, 2]
    targets = jnp.stack([8 * ((y + o) % n_y) + 4 * xl + 2 * core + xh for o in ahead])
    names = jnp.arange(block_order.shape[0])

    def place_of(which):
        return jnp.sum(jnp.where(names[None] == which[:, None], block_order[None], 0), axis=1)

    lags = ((place_of(targets)[:, None] - 1 - place_of(slots)[None]) * tokens).astype(F32).reshape(-1)
    given = pl.pallas_call(
        lambda *refs: pass_on(*refs, n_pieces=len(pieces)),
        in_specs=[SMEM] + [VMEM] * (len(pieces) + 1),
        out_specs=[VMEM] * len(ahead),
        out_shape=[jax.ShapeDtypeStruct(state.shape, F32)] * len(ahead),
    )(lags, *pieces, rates)
    given = [given[0]] + [lax.ppermute(g, "y", around(n_y, o)) for g, o in zip(given[1:], ahead[1:])]

    out_part, given, query_peer = together((out_part, given, query_peer))
    out_parts = [out_part, swap(out_part, "core")]
    n_outs = len(reach) + 1
    full = jax.ShapeDtypeStruct((tokens, out_cols), BF16)
    half_rows = jax.ShapeDtypeStruct((tokens // 2, out_cols), BF16)
    outs = pl.pallas_call(
        lambda *refs: convolve_and_project(*refs, n_given=len(given), n_parts=len(out_parts), n_outs=n_outs),
        in_specs=[SMEM] + [VMEM] * (len(given) + 7) + [HBM] * (1 + len(out_parts)),
        out_specs=[HBM] * n_outs,
        out_shape=[half_rows] * 2 + [full] * (n_outs - 2),
        scratch_shapes=[
            pltpu.VMEM((2 * width // 128, tokens, 128), F32),
            pltpu.VMEM((2 * width // 128, tokens, 128), F32),
            pltpu.VMEM((tokens, 2 * width), BF16),
            pltpu.VMEM(out_weight.shape, BF16),
            pltpu.VMEM(out_weight.shape, BF16),
            pltpu.VMEM((len(reach), tokens, out_cols), BF16),
            pltpu.SemaphoreType.DMA((2 + n_outs,)),
        ],
        compiler_params=params,
    )(
        where_out,
        *given,
        ends,
        mixed,
        query_own,
        query_peer,
        rates,
        gains,
        skip,
        out_weight,
        *out_parts,
    )
    share = dict(zip(reach[1:], outs[2:]))
    low, high = slice(0, tokens // 2), slice(tokens // 2, tokens)

    def add(a, b):
        return (a.astype(F32) + b.astype(F32)).astype(BF16)

    forward = jnp.concatenate([add(ahead_z(outs[0]), share[3][low]), share[3][high]], 0)
    backward = jnp.concatenate([share[-3][low], add(back_z(outs[1]), share[-3][high])], 0)
    for hop in (2, 1):
        forward = add(ahead_z(forward), share[hop])
        backward = add(back_z(backward), share[-hop])
    total = ahead_z(forward).astype(F32) + back_z(backward).astype(F32) + share[0].astype(F32)
    total = total.astype(BF16)
    keep = lax.dynamic_slice_in_dim(total, xh * width, width, 1)
    take = swap(lax.dynamic_slice_in_dim(total, (1 - xh) * width, width, 1))
    first = xh == 0
    return jnp.concatenate([jnp.where(first, keep, take), jnp.where(first, take, keep)], 0)


def solution(mesh):
    ctx, ch = ("y", "xl", "core"), ("z", "xh")
    grid = Mesh(mesh.devices.reshape(4, 2, 2, 8, 2), ctx + ch)
    placed = (
        P(ctx, ch),
        P(None, None, ch),
        P(ch, None),
        P(ch, None),
        P(ch, None),
        P(ch),
        P(),
    )
    return jax.shard_map(
        per_device, mesh=grid, in_specs=placed, out_specs=P(ctx, ch), check_vma=False
    )
```

```python
import jax
import jax.numpy as jnp
from jax import lax
from jax.experimental import pallas as pl
from jax.experimental.pallas import tpu as pltpu
from jax.sharding import Mesh
from jax.sharding import PartitionSpec as P

F32 = jnp.float32
BF16 = jnp.bfloat16
SWAP = [(0, 1), (1, 0)]
ORDER = 16
SEGS = 8
HBM = pl.BlockSpec(memory_space=pltpu.HBM)
SMEM = pl.BlockSpec(memory_space=pltpu.SMEM)
VMEM = pl.BlockSpec()


def around(size, step):
    return [(i, (i + step) % size) for i in range(size)]


GROUP = 4


def project_all(where, *refs, n_chunks):
    chunks = refs[:n_chunks]
    parts, (own, rates, mixed, ends, state, query) = refs[n_chunks : n_chunks + 2], refs[n_chunks + 2 : n_chunks + 8]
    rows, own_rows, peer_rows, own_sums, peer_sums, mixed_rows, sems = refs[n_chunks + 8 :]
    tokens, width = chunks[0].shape
    steps = tokens // SEGS
    for i, chunk in enumerate(chunks):
        pltpu.make_async_copy(chunk, rows.at[where[i]], sems.at[i]).start()
        block = pl.ds(pl.multiple_of(where[i] * width, width), width)
        for k, j in enumerate((1, 2, 0)):
            target = own_rows.at[i, :, pl.ds(k * width, width)]
            pltpu.make_async_copy(own.at[j, block, :], target, sems.at[n_chunks + i]).start()
    for p, part in enumerate(parts):
        blocks = pl.ds(pl.multiple_of(where[n_chunks + p], part.shape[1]), part.shape[1])
        for k in range(part.shape[0]):
            target = peer_rows.at[blocks, :, pl.ds(k * width, width)]
            pltpu.make_async_copy(part.at[k], target, sems.at[2 * n_chunks]).start()

    def own_step(g, _):
        total = None
        for j in range(GROUP):
            i = GROUP * g + j
            pltpu.make_async_copy(rows.at[0], rows.at[0], sems.at[i]).wait()
            pltpu.make_async_copy(own_rows.at[0], own_rows.at[0], sems.at[n_chunks + i]).wait()
            term = jnp.dot(rows[where[i]], own_rows[i], preferred_element_type=F32)
            total = term if total is None else total + term
        own_sums[...] += total
        return 0

    def peer_step(g, _):
        total = None
        for j in range(GROUP):
            term = jnp.dot(rows[GROUP * g + j], peer_rows[GROUP * g + j], preferred_element_type=F32)
            total = term if total is None else total + term
        peer_sums[...] += total
        return 0

    own_sums[...] = jnp.zeros(own_sums.shape, F32)
    peer_sums[...] = jnp.zeros(peer_sums.shape, F32)
    lax.fori_loop(0, n_chunks // GROUP, own_step, 0)
    pltpu.make_async_copy(peer_rows, peer_rows, sems.at[2 * n_chunks]).wait()
    lax.fori_loop(0, n_chunks // GROUP, peer_step, 0)
    for half, sums in enumerate((own_sums, peer_sums)):
        keys, values = sums[:, :width].astype(BF16), sums[:, width : 2 * width].astype(BF16)
        product = (keys.astype(F32) * values.astype(F32)).astype(BF16)
        place = slice(half * width, (half + 1) * width)
        mixed[:, place] = product
        for g in range(width // 128):
            mixed_rows[half * width // 128 + g] = product[:, g * 128 : (g + 1) * 128].astype(F32)
    query[...] = own_sums[:, 2 * width :].astype(BF16)
    fall = jnp.exp(-rates[...])
    later = (SEGS - 1 - lax.broadcasted_iota(jnp.int32, (SEGS, 128), 0)).astype(F32) * float(steps)
    for g in range(2 * width // 128):
        lanes = slice(g * 128, (g + 1) * 128)
        falls = [jnp.broadcast_to(fall[n : n + 1, lanes], (SEGS, 128)) for n in range(ORDER)]

        def step(t, states, g=g, falls=falls):
            now = mixed_rows[g, pl.ds(t, SEGS, stride=steps), :]
            return tuple(f * s + now for f, s in zip(falls, states))

        states = lax.fori_loop(
            0, steps, step, tuple(jnp.zeros((SEGS, 128), F32) for _ in range(ORDER)), unroll=4
        )
        for n in range(ORDER):
            ends[n, :, lanes] = states[n]
            weight = jnp.exp(-rates[n : n + 1, lanes] * later)
            state[n : n + 1, lanes] = jnp.sum(weight * states[n], axis=0, keepdims=True)


def project_query(where, *refs, n_chunks):
    chunks, parts = refs[:n_chunks], refs[n_chunks : n_chunks + 2]
    query, rows, weight_rows, sems = refs[n_chunks + 2 :]
    for p, part in enumerate(parts):
        blocks = pl.ds(pl.multiple_of(where[n_chunks + p], part.shape[1]), part.shape[1])
        pltpu.make_async_copy(part.at[0], weight_rows.at[blocks], sems.at[n_chunks]).start()
    for i, chunk in enumerate(chunks):
        pltpu.make_async_copy(chunk, rows.at[i], sems.at[i]).start()
    pltpu.make_async_copy(weight_rows, weight_rows, sems.at[n_chunks]).wait()
    total = jnp.zeros(query.shape, F32)
    for g in range(0, n_chunks, GROUP):
        for i in range(g, g + GROUP):
            pltpu.make_async_copy(rows.at[i], rows.at[i], sems.at[i]).wait()
        for i in range(g, g + GROUP):
            total += jnp.dot(rows[i], weight_rows[where[i]], preferred_element_type=F32)
    query[...] = total.astype(BF16)


def pass_on(lags, *refs, n_pieces):
    pieces, rates, outs = refs[:n_pieces], refs[n_pieces], refs[n_pieces + 1 :]
    rate = -rates[...]
    per_piece = pieces[0].shape[0]
    for k, out in enumerate(outs):
        total = jnp.zeros(rate.shape, F32)
        for p, piece in enumerate(pieces):
            for i in range(per_piece):
                lag = lags[(k * n_pieces + p) * per_piece + i]
                live = (lag >= 0.0).astype(F32)
                total = total + live * (jnp.exp(rate * jnp.maximum(lag, 0.0)) * piece[i])
        out[...] = total


def convolve(*refs, n_given):
    given = refs[:n_given]
    ends, mixed, query_own, query_peer, rates, gains, skip, gated, mixed_rows, conv_rows = refs[n_given:]
    tokens, width = mixed.shape
    half = width // 2
    steps = tokens // SEGS
    for g in range(width // 128):
        mixed_rows[g] = mixed[:, g * 128 : (g + 1) * 128].astype(F32)
    incoming = given[0][...]
    for more in given[1:]:
        incoming = incoming + more[...]
    rate = rates[...]
    fall = jnp.exp(-rate)
    gain = gains[...]
    order = lax.broadcasted_iota(jnp.int32, (SEGS, 128), 0)
    before = order.astype(F32) * float(steps)
    for g in range(width // 128):
        lanes = slice(g * 128, (g + 1) * 128)
        starts = []
        for n in range(ORDER):
            total = ends[n, :, lanes]
            slow = rate[n : n + 1, lanes]
            for reach in (1, 2, 4):
                moved = jnp.where(order >= reach, pltpu.roll(total, reach, 0), 0.0)
                total = total + jnp.exp(-slow * float(reach * steps)) * moved
            total = jnp.where(order >= 1, pltpu.roll(total, 1, 0), 0.0)
            starts.append(total + jnp.exp(-slow * before) * incoming[n : n + 1, lanes])
        falls = [jnp.broadcast_to(fall[n : n + 1, lanes], (SEGS, 128)) for n in range(ORDER)]
        rises = [jnp.broadcast_to(gain[n : n + 1, lanes], (SEGS, 128)) for n in range(ORDER)]

        def step(t, states, g=g, falls=falls, rises=rises):
            now = mixed_rows[g, pl.ds(t, SEGS, stride=steps), :]
            states = tuple(f * s + now for f, s in zip(falls, states))
            terms = [r * s for r, s in zip(rises, states)]
            while len(terms) > 1:
                terms = [a + b for a, b in zip(terms[::2], terms[1::2])]
            conv_rows[g, pl.ds(t, SEGS, stride=steps), :] = terms[0]
            return states

        lax.fori_loop(0, steps, step, tuple(starts), unroll=2)
        inner = conv_rows[g] + skip[:, lanes] * mixed_rows[g]
        query = (query_own, query_peer)[g * 128 // half]
        gated[:, lanes] = (query[:, g * 128 % half : g * 128 % half + 128].astype(F32) * inner).astype(BF16)


def project_out(where, gated, out_own, *refs, first, n_parts, n_outs):
    parts, outs = refs[:n_parts], refs[n_parts : n_parts + n_outs]
    own_cols, peer_cols, stage, sems = refs[n_parts + n_outs :]
    tokens, half = gated.shape[0], gated.shape[1] // 2
    blocks, cols = stage.shape[0], stage.shape[2]
    deep = parts[0].shape[1]

    def place(i):
        return pl.ds(pl.multiple_of(where[n_parts + first + i] * cols, cols), cols)

    for i in range(blocks):
        pltpu.make_async_copy(out_own.at[:, place(i)], own_cols.at[i], sems.at[0]).start()
    for i, part in enumerate(parts):
        target = peer_cols.at[:, pl.ds(pl.multiple_of(where[i] * deep, deep), deep)]
        pltpu.make_async_copy(part, target, sems.at[1]).start()
    pltpu.make_async_copy(own_cols, own_cols, sems.at[0]).wait()
    pltpu.make_async_copy(peer_cols, peer_cols, sems.at[1]).wait()

    def block(i, _):
        own = jnp.dot(gated[:, :half], own_cols[i], preferred_element_type=F32)
        peer = jnp.dot(gated[:, half:], peer_cols[:, place(i)], preferred_element_type=F32)
        stage[i] = (own + peer).astype(BF16)
        return 0

    copies = []
    if blocks == 1:
        block(0, 0)
        for i, out in enumerate(outs):
            rows = pl.ds(i * (tokens // 2), tokens // 2)
            copies.append(pltpu.make_async_copy(stage.at[0, rows, :], out, sems.at[2 + i]))
            copies[-1].start()
    else:
        for start, stop in ((0, 4), (4, blocks)):
            lax.fori_loop(start, stop, block, 0)
            for i in range(start, stop):
                copies.append(pltpu.make_async_copy(stage.at[i], outs[i], sems.at[2 + i]))
                copies[-1].start()
    for copy in copies:
        copy.wait()


def per_device(hidden_in, in_weight, out_weight, decay, residue, skip_gain, block_order):
    y, xl, core = lax.axis_index("y"), lax.axis_index("xl"), lax.axis_index("core")
    z, xh = lax.axis_index("z"), lax.axis_index("xh")
    n_y, n_z = lax.axis_size("y"), lax.axis_size("z")
    tok_rows, width = hidden_in.shape
    features = in_weight.shape[1]
    tokens = tok_rows // 2

    mine = lax.dynamic_slice_in_dim(hidden_in, xh * tokens, tokens, 0)
    others = lax.dynamic_slice_in_dim(hidden_in, (1 - xh) * tokens, tokens, 0)
    small = jnp.concatenate([decay.T, residue.T, skip_gain[None]], 0)
    out_cols = features // n_z

    def swap(piece, axis="xh"):
        return lax.ppermute(piece, axis, SWAP)

    together = lax.optimization_barrier

    def ahead_z(x):
        return lax.ppermute(x, "z", around(n_z, 1))

    def back_z(x):
        return lax.ppermute(x, "z", around(n_z, -1))

    half, blocks = features // 2, features // 2 // width
    at = core * half
    mixed_part = lax.dynamic_slice(in_weight, (1, at, 0), (2, half, width)).reshape(2, blocks, width, width)
    of1, ob1, p0, small_peer, mixed_part = together(
        (ahead_z(mine), back_z(mine), swap(others), swap(small), mixed_part)
    )
    mixed_part = swap(mixed_part)
    of2, ob2, pf1, pb1 = together((ahead_z(of1), back_z(ob1), ahead_z(p0), back_z(p0)))
    of3, ob3, pf2, pb2 = together((ahead_z(of2), back_z(ob2), ahead_z(pf1), back_z(pb1)))
    of4, pf3, pb3, at = together((ahead_z(of3), ahead_z(pf2), back_z(pb2), at))
    query_part = lax.dynamic_slice(in_weight, (0, at, 0), (1, half, width)).reshape(1, blocks, width, width)
    pb4, mixed_part, query_part, at = together((back_z(pb3), mixed_part, query_part, at))
    query_part = swap(query_part)
    in_parts = [mixed_part, swap(mixed_part, "core")]
    out_part = lax.dynamic_slice_in_dim(out_weight, at, half, 1)
    small = jnp.concatenate([small, small_peer], 1)
    rates, gains, skip = small[:ORDER], small[ORDER : 2 * ORDER], small[2 * ORDER :]
    chunks = [mine, of1, of2, of3, of4, ob1, ob2, ob3, p0, pf1, pf2, pf3, pb1, pb2, pb3, pb4]
    chunk_at = [((z + o) % n_z) * 2 + xh for o in (0, -1, -2, -3, -4, 1, 2, 3)]
    chunk_at += [((z + o) % n_z) * 2 + 1 - xh for o in (0, -1, -2, -3, 1, 2, 3, 4)]
    part_at = [core * blocks, (1 - core) * blocks]
    where = jnp.stack(chunk_at + part_at).astype(jnp.int32)
    reach = [4, -3, 3, 2, -2, 1, -1, 0]
    where_out = jnp.stack([core, 1 - core] + [(z + r) % n_z for r in reach]).astype(jnp.int32)

    params = pltpu.CompilerParams(vmem_limit_bytes=60 << 20)
    mixed, ends, state, query_own = pl.pallas_call(
        lambda *refs: project_all(*refs, n_chunks=len(chunks)),
        in_specs=[SMEM] + [HBM] * (len(chunks) + 3) + [VMEM],
        out_specs=[VMEM] * 4,
        out_shape=[
            jax.ShapeDtypeStruct((tokens, 2 * width), BF16),
            jax.ShapeDtypeStruct((ORDER, SEGS, 2 * width), F32),
            jax.ShapeDtypeStruct((ORDER, 2 * width), F32),
            jax.ShapeDtypeStruct((tokens, width), BF16),
        ],
        scratch_shapes=[
            pltpu.VMEM((len(chunks), tokens, width), BF16),
            pltpu.VMEM((len(chunks), width, 3 * width), BF16),
            pltpu.VMEM((len(chunks), width, 2 * width), BF16),
            pltpu.VMEM((tokens, 3 * width), F32),
            pltpu.VMEM((tokens, 2 * width), F32),
            pltpu.VMEM((2 * width // 128, tokens, 128), F32),
            pltpu.SemaphoreType.DMA((2 * len(chunks) + 1,)),
        ],
        compiler_params=params,
    )(where, *chunks, *in_parts, in_weight, rates)

    pair = jnp.stack([state, lax.ppermute(state, "core", SWAP)])
    turned = jnp.concatenate([pair[:, :, width:], pair[:, :, :width]], 2)
    pieces = [
        pair,
        lax.ppermute(pair, "xl", SWAP),
        lax.ppermute(turned, "xh", SWAP),
        lax.ppermute(turned, ("xl", "xh"), [(0, 3), (3, 0), (1, 2), (2, 1)]),
    ]
    query_part, out_part, pieces = together((query_part, out_part, pieces))
    out_part = swap(out_part)
    query_peer = pl.pallas_call(
        lambda *refs: project_query(*refs, n_chunks=len(chunks)),
        in_specs=[SMEM] + [HBM] * (len(chunks) + 2),
        out_specs=VMEM,
        out_shape=jax.ShapeDtypeStruct((tokens, width), BF16),
        scratch_shapes=[
            pltpu.VMEM((len(chunks), tokens, width), BF16),
            pltpu.VMEM((len(chunks), width, width), BF16),
            pltpu.SemaphoreType.DMA((len(chunks) + 1,)),
        ],
        compiler_params=params,
    )(where, *chunks, query_part, swap(query_part, "core"))
    slots = jnp.stack(
        [
            8 * y + 4 * (xl ^ dl) + 2 * (core ^ dc) + (xh ^ dh)
            for dl, dh in ((0, 0), (1, 0), (0, 1), (1, 1))
            for dc in (0, 1)
        ]
    )
    ahead = [0, 1, -1, 2]
    targets = jnp.stack([8 * ((y + o) % n_y) + 4 * xl + 2 * core + xh for o in ahead])
    names = jnp.arange(block_order.shape[0])

    def place_of(which):
        return jnp.sum(jnp.where(names[None] == which[:, None], block_order[None], 0), axis=1)

    lags = ((place_of(targets)[:, None] - 1 - place_of(slots)[None]) * tokens).astype(F32).reshape(-1)
    given = pl.pallas_call(
        lambda *refs: pass_on(*refs, n_pieces=len(pieces)),
        in_specs=[SMEM] + [VMEM] * (len(pieces) + 1),
        out_specs=[VMEM] * len(ahead),
        out_shape=[jax.ShapeDtypeStruct(state.shape, F32)] * len(ahead),
    )(lags, *pieces, rates)
    given = [given[0]] + [lax.ppermute(g, "y", around(n_y, o)) for g, o in zip(given[1:], ahead[1:])]

    gated = pl.pallas_call(
        lambda *refs: convolve(*refs, n_given=len(given)),
        in_specs=[VMEM] * (len(given) + 7),
        out_specs=VMEM,
        out_shape=jax.ShapeDtypeStruct((tokens, 2 * width), BF16),
        scratch_shapes=[pltpu.VMEM((2 * width // 128, tokens, 128), F32)] * 2,
        compiler_params=params,
    )(*given, ends, mixed, query_own, query_peer, rates, gains, skip)
    out_part, gated = together((out_part, gated))
    out_parts = [out_part, swap(out_part, "core")]

    def project_cols(first, blocks, out_shape):
        return pl.pallas_call(
            lambda *refs: project_out(*refs, first=first, n_parts=len(out_parts), n_outs=len(out_shape)),
            in_specs=[SMEM, VMEM] + [HBM] * (1 + len(out_parts)),
            out_specs=[HBM] * len(out_shape),
            out_shape=out_shape,
            scratch_shapes=[
                pltpu.VMEM((blocks, width, out_cols), BF16),
                pltpu.VMEM(out_weight.shape, BF16),
                pltpu.VMEM((blocks, tokens, out_cols), BF16),
                pltpu.SemaphoreType.DMA((2 + len(out_shape),)),
            ],
            compiler_params=params,
        )(where_out, gated, out_weight, *out_parts)

    farthest = project_cols(0, 1, [jax.ShapeDtypeStruct((tokens // 2, out_cols), BF16)] * 2)
    nearer = project_cols(1, len(reach) - 1, [jax.ShapeDtypeStruct((tokens, out_cols), BF16)] * (len(reach) - 1))
    share = dict(zip(reach[1:], nearer))

    def add(a, b):
        return (a.astype(F32) + b.astype(F32)).astype(BF16)

    forward = add(jnp.pad(ahead_z(farthest[0]).astype(F32), ((0, tokens // 2), (0, 0))), share[3])
    backward = add(jnp.pad(back_z(farthest[1]).astype(F32), ((tokens // 2, 0), (0, 0))), share[-3])
    for hop in (2, 1):
        forward = add(ahead_z(forward), share[hop])
        backward = add(back_z(backward), share[-hop])
    total = ahead_z(forward).astype(F32) + back_z(backward).astype(F32) + share[0].astype(F32)
    total = total.astype(BF16)
    keep = lax.dynamic_slice_in_dim(total, xh * width, width, 1)
    take = swap(lax.dynamic_slice_in_dim(total, (1 - xh) * width, width, 1))
    first = xh == 0
    return jnp.concatenate([jnp.where(first, keep, take), jnp.where(first, take, keep)], 0)


def solution(mesh):
    ctx, ch = ("y", "xl", "core"), ("z", "xh")
    grid = Mesh(mesh.devices.reshape(4, 2, 2, 8, 2), ctx + ch)
    placed = (
        P(ctx, ch),
        P(None, None, ch),
        P(ch, None),
        P(ch, None),
        P(ch, None),
        P(ch),
        P(),
    )
    return jax.shard_map(
        per_device, mesh=grid, in_specs=placed, out_specs=P(ctx, ch), check_vma=False
    )
```

```python
import jax
import jax.numpy as jnp
from jax import lax
from jax.experimental import pallas as pl
from jax.experimental.pallas import tpu as pltpu
from jax.sharding import Mesh
from jax.sharding import PartitionSpec as P

F32 = jnp.float32
BF16 = jnp.bfloat16
SWAP = [(0, 1), (1, 0)]
ORDER = 16
SEGS = 8
HBM = pl.BlockSpec(memory_space=pltpu.HBM)
SMEM = pl.BlockSpec(memory_space=pltpu.SMEM)
VMEM = pl.BlockSpec()


def around(size, step):
    return [(i, (i + step) % size) for i in range(size)]


GROUP = 4


def project_all(where, *refs, n_chunks):
    chunks = refs[:n_chunks]
    parts, (own, rates, mixed, ends, state, query) = refs[n_chunks : n_chunks + 2], refs[n_chunks + 2 : n_chunks + 8]
    rows, own_rows, peer_rows, own_sums, peer_sums, mixed_rows, sems = refs[n_chunks + 8 :]
    tokens, width = chunks[0].shape
    steps = tokens // SEGS
    for i, chunk in enumerate(chunks):
        pltpu.make_async_copy(chunk, rows.at[where[i]], sems.at[i]).start()
        block = pl.ds(pl.multiple_of(where[i] * width, width), width)
        for k, j in enumerate((1, 2, 0)):
            target = own_rows.at[i, :, pl.ds(k * width, width)]
            pltpu.make_async_copy(own.at[j, block, :], target, sems.at[n_chunks + i]).start()
    for p, part in enumerate(parts):
        blocks = pl.ds(pl.multiple_of(where[n_chunks + p], part.shape[1]), part.shape[1])
        for k in range(part.shape[0]):
            target = peer_rows.at[blocks, :, pl.ds(k * width, width)]
            pltpu.make_async_copy(part.at[k], target, sems.at[2 * n_chunks]).start()

    def own_step(g, _):
        total = None
        for j in range(GROUP):
            i = GROUP * g + j
            pltpu.make_async_copy(rows.at[0], rows.at[0], sems.at[i]).wait()
            pltpu.make_async_copy(own_rows.at[0], own_rows.at[0], sems.at[n_chunks + i]).wait()
            term = jnp.dot(rows[where[i]], own_rows[i], preferred_element_type=F32)
            total = term if total is None else total + term
        own_sums[...] += total
        return 0

    def peer_step(g, _):
        total = None
        for j in range(GROUP):
            term = jnp.dot(rows[GROUP * g + j], peer_rows[GROUP * g + j], preferred_element_type=F32)
            total = term if total is None else total + term
        peer_sums[...] += total
        return 0

    own_sums[...] = jnp.zeros(own_sums.shape, F32)
    peer_sums[...] = jnp.zeros(peer_sums.shape, F32)
    lax.fori_loop(0, n_chunks // GROUP, own_step, 0)
    pltpu.make_async_copy(peer_rows, peer_rows, sems.at[2 * n_chunks]).wait()
    lax.fori_loop(0, n_chunks // GROUP, peer_step, 0)
    for half, sums in enumerate((own_sums, peer_sums)):
        keys, values = sums[:, :width].astype(BF16), sums[:, width : 2 * width].astype(BF16)
        product = (keys.astype(F32) * values.astype(F32)).astype(BF16)
        place = slice(half * width, (half + 1) * width)
        mixed[:, place] = product
        for g in range(width // 128):
            mixed_rows[half * width // 128 + g] = product[:, g * 128 : (g + 1) * 128].astype(F32)
    query[...] = own_sums[:, 2 * width :].astype(BF16)
    fall = jnp.exp(-rates[...])
    later = (SEGS - 1 - lax.broadcasted_iota(jnp.int32, (SEGS, 128), 0)).astype(F32) * float(steps)
    for g in range(2 * width // 128):
        lanes = slice(g * 128, (g + 1) * 128)
        falls = [jnp.broadcast_to(fall[n : n + 1, lanes], (SEGS, 128)) for n in range(ORDER)]

        def step(t, states, g=g, falls=falls):
            now = mixed_rows[g, pl.ds(t, SEGS, stride=steps), :]
            return tuple(f * s + now for f, s in zip(falls, states))

        states = lax.fori_loop(
            0, steps, step, tuple(jnp.zeros((SEGS, 128), F32) for _ in range(ORDER)), unroll=4
        )
        for n in range(ORDER):
            ends[n, :, lanes] = states[n]
            weight = jnp.exp(-rates[n : n + 1, lanes] * later)
            state[n : n + 1, lanes] = jnp.sum(weight * states[n], axis=0, keepdims=True)


def project_query(where, *refs, n_chunks):
    chunks, parts = refs[:n_chunks], refs[n_chunks : n_chunks + 2]
    query, rows, weight_rows, sems = refs[n_chunks + 2 :]
    for p, part in enumerate(parts):
        blocks = pl.ds(pl.multiple_of(where[n_chunks + p], part.shape[1]), part.shape[1])
        pltpu.make_async_copy(part.at[0], weight_rows.at[blocks], sems.at[n_chunks]).start()
    for i, chunk in enumerate(chunks):
        pltpu.make_async_copy(chunk, rows.at[i], sems.at[i]).start()
    pltpu.make_async_copy(weight_rows, weight_rows, sems.at[n_chunks]).wait()
    total = jnp.zeros(query.shape, F32)
    for g in range(0, n_chunks, GROUP):
        for i in range(g, g + GROUP):
            pltpu.make_async_copy(rows.at[i], rows.at[i], sems.at[i]).wait()
        for i in range(g, g + GROUP):
            total += jnp.dot(rows[i], weight_rows[where[i]], preferred_element_type=F32)
    query[...] = total.astype(BF16)


def pass_on(lags, *refs, n_pieces):
    pieces, rates, outs = refs[:n_pieces], refs[n_pieces], refs[n_pieces + 1 :]
    rate = -rates[...]
    per_piece = pieces[0].shape[0]
    for k, out in enumerate(outs):
        total = jnp.zeros(rate.shape, F32)
        for p, piece in enumerate(pieces):
            for i in range(per_piece):
                lag = lags[(k * n_pieces + p) * per_piece + i]
                live = (lag >= 0.0).astype(F32)
                total = total + live * (jnp.exp(rate * jnp.maximum(lag, 0.0)) * piece[i])
        out[...] = total


def convolve(*refs, n_given):
    given = refs[:n_given]
    ends, mixed, query_own, query_peer, rates, gains, skip, gated, mixed_rows, conv_rows = refs[n_given:]
    tokens, width = mixed.shape
    half = width // 2
    steps = tokens // SEGS
    for g in range(width // 128):
        mixed_rows[g] = mixed[:, g * 128 : (g + 1) * 128].astype(F32)
    incoming = given[0][...]
    for more in given[1:]:
        incoming = incoming + more[...]
    rate = rates[...]
    fall = jnp.exp(-rate)
    gain = gains[...]
    order = lax.broadcasted_iota(jnp.int32, (SEGS, 128), 0)
    before = order.astype(F32) * float(steps)
    for g in range(width // 128):
        lanes = slice(g * 128, (g + 1) * 128)
        starts = []
        for n in range(ORDER):
            total = ends[n, :, lanes]
            slow = rate[n : n + 1, lanes]
            for reach in (1, 2, 4):
                moved = jnp.where(order >= reach, pltpu.roll(total, reach, 0), 0.0)
                total = total + jnp.exp(-slow * float(reach * steps)) * moved
            total = jnp.where(order >= 1, pltpu.roll(total, 1, 0), 0.0)
            starts.append(total + jnp.exp(-slow * before) * incoming[n : n + 1, lanes])
        falls = [jnp.broadcast_to(fall[n : n + 1, lanes], (SEGS, 128)) for n in range(ORDER)]
        rises = [jnp.broadcast_to(gain[n : n + 1, lanes], (SEGS, 128)) for n in range(ORDER)]

        def step(t, states, g=g, falls=falls, rises=rises):
            now = mixed_rows[g, pl.ds(t, SEGS, stride=steps), :]
            states = tuple(f * s + now for f, s in zip(falls, states))
            terms = [r * s for r, s in zip(rises, states)]
            while len(terms) > 1:
                terms = [a + b for a, b in zip(terms[::2], terms[1::2])]
            conv_rows[g, pl.ds(t, SEGS, stride=steps), :] = terms[0]
            return states

        lax.fori_loop(0, steps, step, tuple(starts), unroll=2)
        inner = conv_rows[g] + skip[:, lanes] * mixed_rows[g]
        query = (query_own, query_peer)[g * 128 // half]
        gated[:, lanes] = (query[:, g * 128 % half : g * 128 % half + 128].astype(F32) * inner).astype(BF16)


def project_out(where, gated, out_own, *refs, first, n_parts, n_outs):
    parts, outs = refs[:n_parts], refs[n_parts : n_parts + n_outs]
    own_cols, peer_cols, stage, sems = refs[n_parts + n_outs :]
    tokens, half = gated.shape[0], gated.shape[1] // 2
    blocks, cols = stage.shape[0], stage.shape[2]
    deep = parts[0].shape[1]

    def place(i):
        return pl.ds(pl.multiple_of(where[n_parts + first + i] * cols, cols), cols)

    for i in range(blocks):
        pltpu.make_async_copy(out_own.at[:, place(i)], own_cols.at[i], sems.at[0]).start()
    for i, part in enumerate(parts):
        target = peer_cols.at[:, pl.ds(pl.multiple_of(where[i] * deep, deep), deep)]
        pltpu.make_async_copy(part, target, sems.at[1]).start()
    pltpu.make_async_copy(own_cols, own_cols, sems.at[0]).wait()
    pltpu.make_async_copy(peer_cols, peer_cols, sems.at[1]).wait()

    def block(i, _):
        own = jnp.dot(gated[:, :half], own_cols[i], preferred_element_type=F32)
        peer = jnp.dot(gated[:, half:], peer_cols[:, place(i)], preferred_element_type=F32)
        stage[i] = (own + peer).astype(BF16)
        return 0

    copies = []
    if blocks == 1:
        block(0, 0)
        for i, out in enumerate(outs):
            rows = pl.ds(i * (tokens // 2), tokens // 2)
            copies.append(pltpu.make_async_copy(stage.at[0, rows, :], out, sems.at[2 + i]))
            copies[-1].start()
    else:
        for start, stop in ((0, 4), (4, blocks)):
            lax.fori_loop(start, stop, block, 0)
            for i in range(start, stop):
                copies.append(pltpu.make_async_copy(stage.at[i], outs[i], sems.at[2 + i]))
                copies[-1].start()
    for copy in copies:
        copy.wait()


def per_device(hidden_in, in_weight, out_weight, decay, residue, skip_gain, block_order):
    y, xl, core = lax.axis_index("y"), lax.axis_index("xl"), lax.axis_index("core")
    z, xh = lax.axis_index("z"), lax.axis_index("xh")
    n_y, n_z = lax.axis_size("y"), lax.axis_size("z")
    tok_rows, width = hidden_in.shape
    features = in_weight.shape[1]
    tokens = tok_rows // 2

    mine = lax.dynamic_slice_in_dim(hidden_in, xh * tokens, tokens, 0)
    others = lax.dynamic_slice_in_dim(hidden_in, (1 - xh) * tokens, tokens, 0)
    small = jnp.concatenate([decay.T, residue.T, skip_gain[None]], 0)
    out_cols = features // n_z

    def swap(piece, axis="xh"):
        return lax.ppermute(piece, axis, SWAP)

    together = lax.optimization_barrier

    def ahead_z(x):
        return lax.ppermute(x, "z", around(n_z, 1))

    def back_z(x):
        return lax.ppermute(x, "z", around(n_z, -1))

    half, blocks = features // 2, features // 2 // width
    at = core * half
    mixed_part = lax.dynamic_slice(in_weight, (1, at, 0), (2, half, width)).reshape(2, blocks, width, width)
    chunk_at = [((z + o) % n_z) * 2 + xh for o in (0, -1, -2, -3, -4, 1, 2, 3)]
    chunk_at += [((z + o) % n_z) * 2 + 1 - xh for o in (0, -1, -2, -3, 1, 2, 3, 4)]
    part_at = [core * blocks, (1 - core) * blocks]
    where = jnp.stack(chunk_at + part_at).astype(jnp.int32)
    reach = [4, -3, 3, 2, -2, 1, -1, 0]
    where_out = jnp.stack([core, 1 - core] + [(z + r) % n_z for r in reach]).astype(jnp.int32)

    slots = jnp.stack(
        [
            8 * y + 4 * (xl ^ dl) + 2 * (core ^ dc) + (xh ^ dh)
            for dl, dh in ((0, 0), (1, 0), (0, 1), (1, 1))
            for dc in (0, 1)
        ]
    )
    ahead = [0, 1, -1, 2]
    targets = jnp.stack([8 * ((y + o) % n_y) + 4 * xl + 2 * core + xh for o in ahead])
    names = jnp.arange(block_order.shape[0])

    def place_of(which):
        return jnp.sum(jnp.where(names[None] == which[:, None], block_order[None], 0), axis=1)

    lags = ((place_of(targets)[:, None] - 1 - place_of(slots)[None]) * tokens).astype(F32).reshape(-1)
    of1, ob1, p0, small_peer, mixed_part = together(
        (ahead_z(mine), back_z(mine), swap(others), swap(small), mixed_part)
    )
    mixed_part = swap(mixed_part)
    of2, ob2, pf1, pb1, where, where_out, lags = together(
        (ahead_z(of1), back_z(ob1), ahead_z(p0), back_z(p0), where, where_out, lags)
    )
    of3, ob3, pf2, pb2 = together((ahead_z(of2), back_z(ob2), ahead_z(pf1), back_z(pb1)))
    of4, pf3, pb3, at = together((ahead_z(of3), ahead_z(pf2), back_z(pb2), at))
    query_part = lax.dynamic_slice(in_weight, (0, at, 0), (1, half, width)).reshape(1, blocks, width, width)
    pb4, mixed_part, query_part, at = together((back_z(pb3), mixed_part, query_part, at))
    query_part = swap(query_part)
    in_parts = [mixed_part, swap(mixed_part, "core")]
    out_part = lax.dynamic_slice_in_dim(out_weight, at, half, 1)
    small = jnp.concatenate([small, small_peer], 1)
    rates, gains, skip = small[:ORDER], small[ORDER : 2 * ORDER], small[2 * ORDER :]
    chunks = [mine, of1, of2, of3, of4, ob1, ob2, ob3, p0, pf1, pf2, pf3, pb1, pb2, pb3, pb4]
    params = pltpu.CompilerParams(vmem_limit_bytes=60 << 20)
    mixed, ends, state, query_own = pl.pallas_call(
        lambda *refs: project_all(*refs, n_chunks=len(chunks)),
        in_specs=[SMEM] + [HBM] * (len(chunks) + 3) + [VMEM],
        out_specs=[VMEM] * 4,
        out_shape=[
            jax.ShapeDtypeStruct((tokens, 2 * width), BF16),
            jax.ShapeDtypeStruct((ORDER, SEGS, 2 * width), F32),
            jax.ShapeDtypeStruct((ORDER, 2 * width), F32),
            jax.ShapeDtypeStruct((tokens, width), BF16),
        ],
        scratch_shapes=[
            pltpu.VMEM((len(chunks), tokens, width), BF16),
            pltpu.VMEM((len(chunks), width, 3 * width), BF16),
            pltpu.VMEM((len(chunks), width, 2 * width), BF16),
            pltpu.VMEM((tokens, 3 * width), F32),
            pltpu.VMEM((tokens, 2 * width), F32),
            pltpu.VMEM((2 * width // 128, tokens, 128), F32),
            pltpu.SemaphoreType.DMA((2 * len(chunks) + 1,)),
        ],
        compiler_params=params,
    )(where, *chunks, *in_parts, in_weight, rates)

    pair = jnp.stack([state, lax.ppermute(state, "core", SWAP)])
    turned = jnp.concatenate([pair[:, :, width:], pair[:, :, :width]], 2)
    pieces = [
        pair,
        lax.ppermute(pair, "xl", SWAP),
        lax.ppermute(turned, "xh", SWAP),
        lax.ppermute(turned, ("xl", "xh"), [(0, 3), (3, 0), (1, 2), (2, 1)]),
    ]
    query_part, out_part, pieces = together((query_part, out_part, pieces))
    out_part = swap(out_part)
    query_peer = pl.pallas_call(
        lambda *refs: project_query(*refs, n_chunks=len(chunks)),
        in_specs=[SMEM] + [HBM] * (len(chunks) + 2),
        out_specs=VMEM,
        out_shape=jax.ShapeDtypeStruct((tokens, width), BF16),
        scratch_shapes=[
            pltpu.VMEM((len(chunks), tokens, width), BF16),
            pltpu.VMEM((len(chunks), width, width), BF16),
            pltpu.SemaphoreType.DMA((len(chunks) + 1,)),
        ],
        compiler_params=params,
    )(where, *chunks, query_part, swap(query_part, "core"))
    given = pl.pallas_call(
        lambda *refs: pass_on(*refs, n_pieces=len(pieces)),
        in_specs=[SMEM] + [VMEM] * (len(pieces) + 1),
        out_specs=[VMEM] * len(ahead),
        out_shape=[jax.ShapeDtypeStruct(state.shape, F32)] * len(ahead),
    )(lags, *pieces, rates)
    given = [given[0]] + [lax.ppermute(g, "y", around(n_y, o)) for g, o in zip(given[1:], ahead[1:])]

    gated = pl.pallas_call(
        lambda *refs: convolve(*refs, n_given=len(given)),
        in_specs=[VMEM] * (len(given) + 7),
        out_specs=VMEM,
        out_shape=jax.ShapeDtypeStruct((tokens, 2 * width), BF16),
        scratch_shapes=[pltpu.VMEM((2 * width // 128, tokens, 128), F32)] * 2,
        compiler_params=params,
    )(*given, ends, mixed, query_own, query_peer, rates, gains, skip)
    out_part, gated = together((out_part, gated))
    out_parts = [out_part, swap(out_part, "core")]

    def project_cols(first, blocks, out_shape):
        return pl.pallas_call(
            lambda *refs: project_out(*refs, first=first, n_parts=len(out_parts), n_outs=len(out_shape)),
            in_specs=[SMEM, VMEM] + [HBM] * (1 + len(out_parts)),
            out_specs=[HBM] * len(out_shape),
            out_shape=out_shape,
            scratch_shapes=[
                pltpu.VMEM((blocks, width, out_cols), BF16),
                pltpu.VMEM(out_weight.shape, BF16),
                pltpu.VMEM((blocks, tokens, out_cols), BF16),
                pltpu.SemaphoreType.DMA((2 + len(out_shape),)),
            ],
            compiler_params=params,
        )(where_out, gated, out_weight, *out_parts)

    farthest = project_cols(0, 1, [jax.ShapeDtypeStruct((tokens // 2, out_cols), BF16)] * 2)
    nearer = project_cols(1, len(reach) - 1, [jax.ShapeDtypeStruct((tokens, out_cols), BF16)] * (len(reach) - 1))
    share = dict(zip(reach[1:], nearer))

    def add(a, b):
        return (a.astype(F32) + b.astype(F32)).astype(BF16)

    forward = add(jnp.pad(ahead_z(farthest[0]).astype(F32), ((0, tokens // 2), (0, 0))), share[3])
    backward = add(jnp.pad(back_z(farthest[1]).astype(F32), ((tokens // 2, 0), (0, 0))), share[-3])
    for hop in (2, 1):
        forward = add(ahead_z(forward), share[hop])
        backward = add(back_z(backward), share[-hop])
    total = ahead_z(forward).astype(F32) + back_z(backward).astype(F32) + share[0].astype(F32)
    total = total.astype(BF16)
    keep = lax.dynamic_slice_in_dim(total, xh * width, width, 1)
    take = swap(lax.dynamic_slice_in_dim(total, (1 - xh) * width, width, 1))
    first = xh == 0
    return jnp.concatenate([jnp.where(first, keep, take), jnp.where(first, take, keep)], 0)


def solution(mesh):
    ctx, ch = ("y", "xl", "core"), ("z", "xh")
    grid = Mesh(mesh.devices.reshape(4, 2, 2, 8, 2), ctx + ch)
    placed = (
        P(ctx, ch),
        P(None, None, ch),
        P(ch, None),
        P(ch, None),
        P(ch, None),
        P(ch),
        P(),
    )
    return jax.shard_map(
        per_device, mesh=grid, in_specs=placed, out_specs=P(ctx, ch), check_vma=False
    )
```

```python
import jax
import jax.numpy as jnp
from jax import lax
from jax.experimental import pallas as pl
from jax.experimental.pallas import tpu as pltpu
from jax.sharding import Mesh
from jax.sharding import PartitionSpec as P

F32 = jnp.float32
BF16 = jnp.bfloat16
SWAP = [(0, 1), (1, 0)]
ORDER = 16
SEGS = 8
HBM = pl.BlockSpec(memory_space=pltpu.HBM)
SMEM = pl.BlockSpec(memory_space=pltpu.SMEM)
VMEM = pl.BlockSpec()


def around(size, step):
    return [(i, (i + step) % size) for i in range(size)]


GROUP = 4


def project_all(where, *refs, n_chunks):
    chunks = refs[:n_chunks]
    parts, (own, rates, mixed, ends, state, query) = refs[n_chunks : n_chunks + 2], refs[n_chunks + 2 : n_chunks + 8]
    rows, own_rows, peer_rows, own_sums, peer_sums, mixed_rows, sems = refs[n_chunks + 8 :]
    tokens, width = chunks[0].shape
    steps = tokens // SEGS
    for i, chunk in enumerate(chunks):
        pltpu.make_async_copy(chunk, rows.at[where[i]], sems.at[i]).start()
        block = pl.ds(pl.multiple_of(where[i] * width, width), width)
        for k, j in enumerate((1, 2, 0)):
            target = own_rows.at[i, :, pl.ds(k * width, width)]
            pltpu.make_async_copy(own.at[j, block, :], target, sems.at[n_chunks + i]).start()
    for p, part in enumerate(parts):
        blocks = pl.ds(pl.multiple_of(where[n_chunks + p], part.shape[1]), part.shape[1])
        for k in range(part.shape[0]):
            target = peer_rows.at[blocks, :, pl.ds(k * width, width)]
            pltpu.make_async_copy(part.at[k], target, sems.at[2 * n_chunks]).start()

    def own_step(g, _):
        total = None
        for j in range(GROUP):
            i = GROUP * g + j
            pltpu.make_async_copy(rows.at[0], rows.at[0], sems.at[i]).wait()
            pltpu.make_async_copy(own_rows.at[0], own_rows.at[0], sems.at[n_chunks + i]).wait()
            term = jnp.dot(rows[where[i]], own_rows[i], preferred_element_type=F32)
            total = term if total is None else total + term
        own_sums[...] += total
        return 0

    def peer_step(g, _):
        total = None
        for j in range(2 * GROUP):
            term = jnp.dot(rows[2 * GROUP * g + j], peer_rows[2 * GROUP * g + j], preferred_element_type=F32)
            total = term if total is None else total + term
        peer_sums[...] += total
        return 0

    own_sums[...] = jnp.zeros(own_sums.shape, F32)
    peer_sums[...] = jnp.zeros(peer_sums.shape, F32)
    lax.fori_loop(0, n_chunks // GROUP, own_step, 0)
    pltpu.make_async_copy(peer_rows, peer_rows, sems.at[2 * n_chunks]).wait()
    lax.fori_loop(0, n_chunks // (2 * GROUP), peer_step, 0)
    for half, sums in enumerate((own_sums, peer_sums)):
        keys, values = sums[:, :width].astype(BF16), sums[:, width : 2 * width].astype(BF16)
        product = (keys.astype(F32) * values.astype(F32)).astype(BF16)
        place = slice(half * width, (half + 1) * width)
        mixed[:, place] = product
        for g in range(width // 128):
            mixed_rows[half * width // 128 + g] = product[:, g * 128 : (g + 1) * 128].astype(F32)
    query[...] = own_sums[:, 2 * width :].astype(BF16)
    fall = jnp.exp(-rates[...])
    later = (SEGS - 1 - lax.broadcasted_iota(jnp.int32, (SEGS, 128), 0)).astype(F32) * float(steps)
    for g in range(2 * width // 128):
        lanes = slice(g * 128, (g + 1) * 128)
        falls = [jnp.broadcast_to(fall[n : n + 1, lanes], (SEGS, 128)) for n in range(ORDER)]

        def step(t, states, g=g, falls=falls):
            now = mixed_rows[g, pl.ds(t, SEGS, stride=steps), :]
            return tuple(f * s + now for f, s in zip(falls, states))

        states = lax.fori_loop(
            0, steps, step, tuple(jnp.zeros((SEGS, 128), F32) for _ in range(ORDER)), unroll=8
        )
        for n in range(ORDER):
            ends[n, :, lanes] = states[n]
            weight = jnp.exp(-rates[n : n + 1, lanes] * later)
            state[n : n + 1, lanes] = jnp.sum(weight * states[n], axis=0, keepdims=True)


def project_query(where, *refs, n_chunks):
    chunks, parts = refs[:n_chunks], refs[n_chunks : n_chunks + 2]
    query, rows, weight_rows, sems = refs[n_chunks + 2 :]
    for p, part in enumerate(parts):
        blocks = pl.ds(pl.multiple_of(where[n_chunks + p], part.shape[1]), part.shape[1])
        pltpu.make_async_copy(part.at[0], weight_rows.at[blocks], sems.at[n_chunks]).start()
    for i, chunk in enumerate(chunks):
        pltpu.make_async_copy(chunk, rows.at[i], sems.at[i]).start()
    pltpu.make_async_copy(weight_rows, weight_rows, sems.at[n_chunks]).wait()
    total = jnp.zeros(query.shape, F32)
    for g in range(0, n_chunks, GROUP):
        for i in range(g, g + GROUP):
            pltpu.make_async_copy(rows.at[i], rows.at[i], sems.at[i]).wait()
        for i in range(g, g + GROUP):
            total += jnp.dot(rows[i], weight_rows[where[i]], preferred_element_type=F32)
    query[...] = total.astype(BF16)


def pass_on(lags, *refs, n_pieces):
    pieces, rates, outs = refs[:n_pieces], refs[n_pieces], refs[n_pieces + 1 :]
    rate = -rates[...]
    per_piece = pieces[0].shape[0]
    for k, out in enumerate(outs):
        total = jnp.zeros(rate.shape, F32)
        for p, piece in enumerate(pieces):
            for i in range(per_piece):
                lag = lags[(k * n_pieces + p) * per_piece + i]
                live = (lag >= 0.0).astype(F32)
                total = total + live * (jnp.exp(rate * jnp.maximum(lag, 0.0)) * piece[i])
        out[...] = total


def convolve(*refs, n_given):
    given = refs[:n_given]
    ends, mixed, query_own, query_peer, rates, gains, skip, gated, mixed_rows, conv_rows = refs[n_given:]
    tokens, width = mixed.shape
    half = width // 2
    steps = tokens // SEGS
    for g in range(width // 128):
        mixed_rows[g] = mixed[:, g * 128 : (g + 1) * 128].astype(F32)
    incoming = given[0][...]
    for more in given[1:]:
        incoming = incoming + more[...]
    rate = rates[...]
    fall = jnp.exp(-rate)
    gain = gains[...]
    order = lax.broadcasted_iota(jnp.int32, (SEGS, 128), 0)
    before = order.astype(F32) * float(steps)
    for g in range(width // 128):
        lanes = slice(g * 128, (g + 1) * 128)
        starts = []
        for n in range(ORDER):
            total = ends[n, :, lanes]
            slow = rate[n : n + 1, lanes]
            for reach in (1, 2, 4):
                moved = jnp.where(order >= reach, pltpu.roll(total, reach, 0), 0.0)
                total = total + jnp.exp(-slow * float(reach * steps)) * moved
            total = jnp.where(order >= 1, pltpu.roll(total, 1, 0), 0.0)
            starts.append(total + jnp.exp(-slow * before) * incoming[n : n + 1, lanes])
        falls = [jnp.broadcast_to(fall[n : n + 1, lanes], (SEGS, 128)) for n in range(ORDER)]
        rises = [jnp.broadcast_to(gain[n : n + 1, lanes], (SEGS, 128)) for n in range(ORDER)]

        def step(t, states, g=g, falls=falls, rises=rises):
            now = mixed_rows[g, pl.ds(t, SEGS, stride=steps), :]
            states = tuple(f * s + now for f, s in zip(falls, states))
            terms = [r * s for r, s in zip(rises, states)]
            while len(terms) > 1:
                terms = [a + b for a, b in zip(terms[::2], terms[1::2])]
            conv_rows[g, pl.ds(t, SEGS, stride=steps), :] = terms[0]
            return states

        lax.fori_loop(0, steps, step, tuple(starts), unroll=2)
        inner = conv_rows[g] + skip[:, lanes] * mixed_rows[g]
        query = (query_own, query_peer)[g * 128 // half]
        gated[:, lanes] = (query[:, g * 128 % half : g * 128 % half + 128].astype(F32) * inner).astype(BF16)


def project_out(where, gated, out_own, *refs, first, n_parts, n_outs):
    parts, outs = refs[:n_parts], refs[n_parts : n_parts + n_outs]
    own_cols, peer_cols, stage, sems = refs[n_parts + n_outs :]
    tokens, half = gated.shape[0], gated.shape[1] // 2
    blocks, cols = stage.shape[0], stage.shape[2]
    deep = parts[0].shape[1]

    def place(i):
        return pl.ds(pl.multiple_of(where[n_parts + first + i] * cols, cols), cols)

    for i in range(blocks):
        pltpu.make_async_copy(out_own.at[:, place(i)], own_cols.at[i], sems.at[0]).start()
    for i, part in enumerate(parts):
        target = peer_cols.at[:, pl.ds(pl.multiple_of(where[i] * deep, deep), deep)]
        pltpu.make_async_copy(part, target, sems.at[1]).start()
    pltpu.make_async_copy(own_cols, own_cols, sems.at[0]).wait()
    pltpu.make_async_copy(peer_cols, peer_cols, sems.at[1]).wait()

    def block(i, _):
        own = jnp.dot(gated[:, :half], own_cols[i], preferred_element_type=F32)
        peer = jnp.dot(gated[:, half:], peer_cols[:, place(i)], preferred_element_type=F32)
        stage[i] = (own + peer).astype(BF16)
        return 0

    copies = []
    if blocks == 1:
        block(0, 0)
        for i, out in enumerate(outs):
            rows = pl.ds(i * (tokens // 2), tokens // 2)
            copies.append(pltpu.make_async_copy(stage.at[0, rows, :], out, sems.at[2 + i]))
            copies[-1].start()
    else:
        for start, stop in ((0, 4), (4, blocks)):
            lax.fori_loop(start, stop, block, 0)
            for i in range(start, stop):
                copies.append(pltpu.make_async_copy(stage.at[i], outs[i], sems.at[2 + i]))
                copies[-1].start()
    for copy in copies:
        copy.wait()


def per_device(hidden_in, in_weight, out_weight, decay, residue, skip_gain, block_order):
    y, xl, core = lax.axis_index("y"), lax.axis_index("xl"), lax.axis_index("core")
    z, xh = lax.axis_index("z"), lax.axis_index("xh")
    n_y, n_z = lax.axis_size("y"), lax.axis_size("z")
    tok_rows, width = hidden_in.shape
    features = in_weight.shape[1]
    tokens = tok_rows // 2

    mine = lax.dynamic_slice_in_dim(hidden_in, xh * tokens, tokens, 0)
    others = lax.dynamic_slice_in_dim(hidden_in, (1 - xh) * tokens, tokens, 0)
    small = jnp.concatenate([decay.T, residue.T, skip_gain[None]], 0)
    out_cols = features // n_z

    def swap(piece, axis="xh"):
        return lax.ppermute(piece, axis, SWAP)

    together = lax.optimization_barrier

    def ahead_z(x):
        return lax.ppermute(x, "z", around(n_z, 1))

    def back_z(x):
        return lax.ppermute(x, "z", around(n_z, -1))

    half, blocks = features // 2, features // 2 // width
    at = core * half
    mixed_part = lax.dynamic_slice(in_weight, (1, at, 0), (2, half, width)).reshape(2, blocks, width, width)
    chunk_at = [((z + o) % n_z) * 2 + xh for o in (0, -1, -2, -3, -4, 1, 2, 3)]
    chunk_at += [((z + o) % n_z) * 2 + 1 - xh for o in (0, -1, -2, -3, 1, 2, 3, 4)]
    part_at = [core * blocks, (1 - core) * blocks]
    where = jnp.stack(chunk_at + part_at).astype(jnp.int32)
    reach = [4, -3, 3, 2, -2, 1, -1, 0]
    where_out = jnp.stack([core, 1 - core] + [(z + r) % n_z for r in reach]).astype(jnp.int32)

    slots = jnp.stack(
        [
            8 * y + 4 * (xl ^ dl) + 2 * (core ^ dc) + (xh ^ dh)
            for dl, dh in ((0, 0), (1, 0), (0, 1), (1, 1))
            for dc in (0, 1)
        ]
    )
    ahead = [0, 1, -1, 2]
    targets = jnp.stack([8 * ((y + o) % n_y) + 4 * xl + 2 * core + xh for o in ahead])
    names = jnp.arange(block_order.shape[0])

    def place_of(which):
        return jnp.sum(jnp.where(names[None] == which[:, None], block_order[None], 0), axis=1)

    lags = ((place_of(targets)[:, None] - 1 - place_of(slots)[None]) * tokens).astype(F32).reshape(-1)
    of1, ob1, p0, small_peer, mixed_part = together(
        (ahead_z(mine), back_z(mine), swap(others), swap(small), mixed_part)
    )
    mixed_part = swap(mixed_part)
    of2, ob2, pf1, pb1, where, where_out, lags = together(
        (ahead_z(of1), back_z(ob1), ahead_z(p0), back_z(p0), where, where_out, lags)
    )
    of3, ob3, pf2, pb2 = together((ahead_z(of2), back_z(ob2), ahead_z(pf1), back_z(pb1)))
    of4, pf3, pb3, at = together((ahead_z(of3), ahead_z(pf2), back_z(pb2), at))
    query_part = lax.dynamic_slice(in_weight, (0, at, 0), (1, half, width)).reshape(1, blocks, width, width)
    pb4, mixed_part, query_part, at = together((back_z(pb3), mixed_part, query_part, at))
    query_part = swap(query_part)
    in_parts = [mixed_part, swap(mixed_part, "core")]
    out_part = lax.dynamic_slice_in_dim(out_weight, at, half, 1)
    small = jnp.concatenate([small, small_peer], 1)
    rates, gains, skip = small[:ORDER], small[ORDER : 2 * ORDER], small[2 * ORDER :]
    chunks = [mine, of1, of2, of3, of4, ob1, ob2, ob3, p0, pf1, pf2, pf3, pb1, pb2, pb3, pb4]
    params = pltpu.CompilerParams(vmem_limit_bytes=60 << 20)
    mixed, ends, state, query_own = pl.pallas_call(
        lambda *refs: project_all(*refs, n_chunks=len(chunks)),
        in_specs=[SMEM] + [HBM] * (len(chunks) + 3) + [VMEM],
        out_specs=[VMEM] * 4,
        out_shape=[
            jax.ShapeDtypeStruct((tokens, 2 * width), BF16),
            jax.ShapeDtypeStruct((ORDER, SEGS, 2 * width), F32),
            jax.ShapeDtypeStruct((ORDER, 2 * width), F32),
            jax.ShapeDtypeStruct((tokens, width), BF16),
        ],
        scratch_shapes=[
            pltpu.VMEM((len(chunks), tokens, width), BF16),
            pltpu.VMEM((len(chunks), width, 3 * width), BF16),
            pltpu.VMEM((len(chunks), width, 2 * width), BF16),
            pltpu.VMEM((tokens, 3 * width), F32),
            pltpu.VMEM((tokens, 2 * width), F32),
            pltpu.VMEM((2 * width // 128, tokens, 128), F32),
            pltpu.SemaphoreType.DMA((2 * len(chunks) + 1,)),
        ],
        compiler_params=params,
    )(where, *chunks, *in_parts, in_weight, rates)

    pair = jnp.stack([state, lax.ppermute(state, "core", SWAP)])
    turned = jnp.concatenate([pair[:, :, width:], pair[:, :, :width]], 2)
    pieces = [
        pair,
        lax.ppermute(pair, "xl", SWAP),
        lax.ppermute(turned, "xh", SWAP),
        lax.ppermute(turned, ("xl", "xh"), [(0, 3), (3, 0), (1, 2), (2, 1)]),
    ]
    query_part, out_part, pieces = together((query_part, out_part, pieces))
    out_part = swap(out_part)
    query_peer = pl.pallas_call(
        lambda *refs: project_query(*refs, n_chunks=len(chunks)),
        in_specs=[SMEM] + [HBM] * (len(chunks) + 2),
        out_specs=VMEM,
        out_shape=jax.ShapeDtypeStruct((tokens, width), BF16),
        scratch_shapes=[
            pltpu.VMEM((len(chunks), tokens, width), BF16),
            pltpu.VMEM((len(chunks), width, width), BF16),
            pltpu.SemaphoreType.DMA((len(chunks) + 1,)),
        ],
        compiler_params=params,
    )(where, *chunks, query_part, swap(query_part, "core"))
    given = pl.pallas_call(
        lambda *refs: pass_on(*refs, n_pieces=len(pieces)),
        in_specs=[SMEM] + [VMEM] * (len(pieces) + 1),
        out_specs=[VMEM] * len(ahead),
        out_shape=[jax.ShapeDtypeStruct(state.shape, F32)] * len(ahead),
    )(lags, *pieces, rates)
    given = [given[0]] + [lax.ppermute(g, "y", around(n_y, o)) for g, o in zip(given[1:], ahead[1:])]

    gated = pl.pallas_call(
        lambda *refs: convolve(*refs, n_given=len(given)),
        in_specs=[VMEM] * (len(given) + 7),
        out_specs=VMEM,
        out_shape=jax.ShapeDtypeStruct((tokens, 2 * width), BF16),
        scratch_shapes=[pltpu.VMEM((2 * width // 128, tokens, 128), F32)] * 2,
        compiler_params=params,
    )(*given, ends, mixed, query_own, query_peer, rates, gains, skip)
    out_part, gated = together((out_part, gated))
    out_parts = [out_part, swap(out_part, "core")]

    def project_cols(first, blocks, out_shape):
        return pl.pallas_call(
            lambda *refs: project_out(*refs, first=first, n_parts=len(out_parts), n_outs=len(out_shape)),
            in_specs=[SMEM, VMEM] + [HBM] * (1 + len(out_parts)),
            out_specs=[HBM] * len(out_shape),
            out_shape=out_shape,
            scratch_shapes=[
                pltpu.VMEM((blocks, width, out_cols), BF16),
                pltpu.VMEM(out_weight.shape, BF16),
                pltpu.VMEM((blocks, tokens, out_cols), BF16),
                pltpu.SemaphoreType.DMA((2 + len(out_shape),)),
            ],
            compiler_params=params,
        )(where_out, gated, out_weight, *out_parts)

    farthest = project_cols(0, 1, [jax.ShapeDtypeStruct((tokens // 2, out_cols), BF16)] * 2)
    nearer = project_cols(1, len(reach) - 1, [jax.ShapeDtypeStruct((tokens, out_cols), BF16)] * (len(reach) - 1))
    share = dict(zip(reach[1:], nearer))

    def add(a, b):
        return (a.astype(F32) + b.astype(F32)).astype(BF16)

    forward = add(jnp.pad(ahead_z(farthest[0]).astype(F32), ((0, tokens // 2), (0, 0))), share[3])
    backward = add(jnp.pad(back_z(farthest[1]).astype(F32), ((tokens // 2, 0), (0, 0))), share[-3])
    for hop in (2, 1):
        forward = add(ahead_z(forward), share[hop])
        backward = add(back_z(backward), share[-hop])
    total = ahead_z(forward).astype(F32) + back_z(backward).astype(F32) + share[0].astype(F32)
    total = total.astype(BF16)
    keep = lax.dynamic_slice_in_dim(total, xh * width, width, 1)
    take = swap(lax.dynamic_slice_in_dim(total, (1 - xh) * width, width, 1))
    first = xh == 0
    return jnp.concatenate([jnp.where(first, keep, take), jnp.where(first, take, keep)], 0)


def solution(mesh):
    ctx, ch = ("y", "xl", "core"), ("z", "xh")
    grid = Mesh(mesh.devices.reshape(4, 2, 2, 8, 2), ctx + ch)
    placed = (
        P(ctx, ch),
        P(None, None, ch),
        P(ch, None),
        P(ch, None),
        P(ch, None),
        P(ch),
        P(),
    )
    return jax.shard_map(
        per_device, mesh=grid, in_specs=placed, out_specs=P(ctx, ch), check_vma=False
    )
```
